32 devices in a mesh: rep: 8 (over z, x), grp: 4 (over y, core).
Axes of the slice: x: 2, y: 2, z: 4, core: 2. Of those that a mesh axis runs over, the one named last changes fastest.
Arguments:
- images: bfloat16 [32, 14, 14, 512], P(('rep', 'grp')), may hold values from -45 to 45
- cotangent: bfloat16 [32, 14, 14, 512], P(('rep', 'grp')), may hold values from -6 to 6
- region_ids: int32 [14, 14], replicated, may hold values from 0 to 8, as said below
- rel_index: int32 [169], replicated, may hold values from 0 to 168, each once
- matrices: float32 [3145728], P(('rep', 'grp')), may hold values from -0.8838835 to 0.8838835
- matrix_m: float32 [3145728], P(('rep', 'grp')), may hold values from -0.75 to 0.75
- matrix_v: float32 [3145728], P(('rep', 'grp')), may hold values from 2e-05 to 0.0005
- small: float32 [8848], replicated, may hold values from -4 to 301.5
- small_m: float32 [8848], replicated, may hold values from -0.75 to 0.75
- small_v: float32 [8848], replicated, may hold values from 2e-05 to 0.0005
Outputs:
- output: bfloat16 [32, 14, 14, 512], P(('rep', 'grp'))
- input_grad: bfloat16 [32, 14, 14, 512], P(('rep', 'grp'))
- matrix_grad: float32 [3145728], P(('rep', 'grp'))
- small_grad: float32 [8848], replicated
- new_matrices: float32 [3145728], P(('rep', 'grp'))
- new_matrix_m: float32 [3145728], P(('rep', 'grp'))
- new_matrix_v: float32 [3145728], P(('rep', 'grp'))
- new_small: float32 [8848], replicated
- new_small_m: float32 [8848], replicated
- new_small_v: float32 [8848], replicated
The draws below stay inside these ranges and needn't reach their ends.
Inputs may be any that keep to these rules, and one draw needn't show every extreme that they name: `region_ids`: 3 times a row band plus a column band; each dimension is cut into three nonempty bands. `rel_index`: a permutation of the table's rows.
All inputs are finite; a program needn't handle non-finite values.
Results may differ from the reference program's by a relative error of at most 0.01.
The reference program's roundings to bfloat16 on the way count: a program that leaves them out, or rounds other values in their place, can miss the bound.
Values may be sent and summed in bfloat16 or wider, within the bound.
No kernel may reach another device: no remote copies, remote signals or barrier semaphores. Data moves between devices by JAX's collectives and lax.ppermute only.
A program may use at most 128 MiB of HBM per device.

```python
import math
import jax
import jax.numpy as jnp
from jax import lax

D = 512
HEADS = 16
FF = 2048
WIN = 7
SIDE = 14
SHIFT = 3
STEP = 5
HEAD_DIM = 32
REL = 169
IMAGES = 32
TOKENS = 6272
MAT = 3145728
SMALL = 8848
N_REP = 8


def draw_images(key, part):
    key_base, key_token, key_feature = jax.random.split(key, 3)
    shape = (IMAGES, SIDE, SIDE, D)
    token_scale = 0.3 * jnp.exp(jax.random.uniform(key_token, (IMAGES, SIDE, SIDE, 1), jnp.float32, 0.0, math.log(10.0)))
    feature_scale = 0.3 * jnp.exp(jax.random.uniform(key_feature, (D,), jnp.float32, 0.0, math.log(10.0)))
    base = jnp.clip(jax.random.normal(key_base, shape, jnp.float32), -5.0, 5.0)
    return (base * token_scale * feature_scale).astype(jnp.bfloat16)


def band_cuts(key):
    key_lower, key_upper = jax.random.split(key)
    lower = jax.random.randint(key_lower, (), 1, SIDE - 1)
    upper = jax.random.randint(key_upper, (), lower + 1, SIDE)
    return (lower, upper)


def draw_region_ids(key, part):
    key_rows, key_cols = jax.random.split(key)
    row_lower, row_upper = band_cuts(key_rows)
    col_lower, col_upper = band_cuts(key_cols)
    spots = jnp.arange(SIDE, dtype=jnp.int32)
    row_band = (spots >= row_lower).astype(jnp.int32) + (spots >= row_upper).astype(jnp.int32)
    col_band = (spots >= col_lower).astype(jnp.int32) + (spots >= col_upper).astype(jnp.int32)
    return 3 * row_band[:, None] + col_band[None, :]


def draw_matrices(key, part):
    bound_one = 3 * D * D
    bound_two = bound_one + D * D
    bound_three = bound_two + D * FF
    spots = jnp.arange(MAT, dtype=jnp.int32)
    scales = jnp.where(spots < bound_one, D ** (-0.5), jnp.where(spots < bound_two, 4.0 * D ** (-0.5), jnp.where(spots < bound_three, D ** (-0.5), FF ** (-0.5))))
    base = jnp.clip(jax.random.normal(key, (MAT,), jnp.float32), -5.0, 5.0)
    return (base * scales).astype(jnp.float32)


def draw_small(key, part):
    keys = jax.random.split(key, 3)
    gains = 1.0 + 0.15 * jax.random.uniform(keys[0], (2 * D,), jnp.float32, -1.0, 1.0)
    shifts = 0.3 * jnp.clip(jax.random.normal(keys[1], (6 * D + FF,), jnp.float32), -5.0, 5.0)
    table = jnp.clip(jax.random.normal(keys[2], (REL, HEADS), jnp.float32), -4.0, 4.0)
    return jnp.concatenate([gains, shifts, table.reshape(-1)]).astype(jnp.float32)


def shard_levels(own_key, shape, cuts, smallest, high):
    def one(position, blocks):
        heights = jax.random.uniform(jax.random.fold_in(jax.random.fold_in(own_key, 6), position), (blocks,), jnp.float32, smallest / len(cuts), high / len(cuts))
        return jnp.repeat(jnp.exp(heights), shape[position] // blocks).reshape((-1,) + (1,) * (len(shape) - position - 1))

    level = one(*cuts[0])
    for cut in cuts[1:]:
        level = level * one(*cut)
    return level


def noise(key, shape, width, limit, cuts=(), kind=jnp.bfloat16):
    values = jax.random.normal(key, shape, jnp.float32) * width
    if len(cuts) > 0:
        values = shard_levels(key, shape, cuts, -0.22, 0.18) * values
    return jnp.clip(values, min=-limit, max=limit).astype(kind)


def setup_inputs(seed: int = 0) -> dict:
    key_list = jax.random.split(jax.random.key(seed), 11)
    images = draw_images(jax.random.fold_in(key_list[10], 71), 0)
    cotangent = noise(key_list[1], (IMAGES, SIDE, SIDE, D), 1.0, 6.0, ((0, 32),))
    region_ids = draw_region_ids(jax.random.fold_in(key_list[10], 71), 0)
    rel_index = jax.random.permutation(key_list[3], REL).astype(jnp.int32)
    matrices = draw_matrices(jax.random.fold_in(key_list[10], 71), 0)
    matrix_m = noise(key_list[5], (MAT,), 0.05, 0.75, ((0, 32),), jnp.float32)
    matrix_v = jnp.clip(jnp.exp(math.log(0.0005) - 3.218876 * jax.random.uniform(key_list[6], (MAT,), jnp.float32) ** shard_levels(key_list[6], (MAT,), ((0, 32),), -0.2, 0.2)), 1.9999999494757503e-05, 0.0005)
    small = draw_small(jax.random.fold_in(key_list[10], 71), 0)
    small_m = noise(key_list[8], (SMALL,), 0.05, 0.75, (), jnp.float32)
    small_v = jnp.clip(jnp.exp(jax.random.uniform(key_list[9], (SMALL,), jnp.float32, math.log(1.9999999494757503e-05), math.log(0.0005))), 1.9999999494757503e-05, 0.0005)
    return dict(images=images, cotangent=cotangent, region_ids=region_ids, rel_index=rel_index, matrices=matrices, matrix_m=matrix_m, matrix_v=matrix_v, small=small, small_m=small_m, small_v=small_v)


norm_eps = 1e-05
beta_one = 0.9
beta_two = 0.999
adam_eps = 1e-08
rate_matrix = 0.01
rate_small = 0.2
decay_rate = 0.05
masked_score = -1e+30
root_half = 0.7071067811865476
inv_root_twopi = 0.3989422804014327
highest = lax.Precision.HIGHEST

def rounded(values):
    return lax.optimization_barrier(values.astype(jnp.bfloat16))

def norm_stats(values):
    center = values - lax.optimization_barrier(jnp.mean(values, axis=-1, keepdims=True))
    spread = lax.optimization_barrier(jnp.mean(center * center, axis=-1, keepdims=True))
    scaling = lax.rsqrt(spread + norm_eps)
    return (center * scaling, scaling)

def norm_back(incoming, normed, scaling, gain_vector):
    scaled = incoming * gain_vector
    backward = scaling * (scaled - lax.optimization_barrier(jnp.mean(scaled, axis=-1, keepdims=True)) - normed * lax.optimization_barrier(jnp.mean(scaled * normed, axis=-1, keepdims=True)))
    return (backward, lax.optimization_barrier(jnp.sum(incoming * normed, axis=(0, 1, 2))), lax.optimization_barrier(jnp.sum(incoming, axis=(0, 1, 2))))

def gelu_slope(values):
    return 0.5 * (1.0 + lax.erf(values * root_half)) + values * jnp.exp(-0.5 * values * values) * inv_root_twopi

def to_windows(spatial):
    image_count = spatial.shape[0]
    blocks = SIDE // WIN
    rolled = jnp.roll(spatial, (-SHIFT, -SHIFT), axis=(1, 2))
    blocked = rolled.reshape(image_count, blocks, WIN, blocks, WIN, spatial.shape[-1])
    return blocked.transpose(0, 1, 3, 2, 4, 5).reshape(image_count, blocks * blocks, WIN * WIN, spatial.shape[-1])

def from_windows(window_grid):
    image_count = window_grid.shape[0]
    blocks = SIDE // WIN
    blocked = window_grid.reshape(image_count, blocks, blocks, WIN, WIN, window_grid.shape[-1])
    spatial = blocked.transpose(0, 1, 3, 2, 4, 5).reshape(image_count, SIDE, SIDE, window_grid.shape[-1])
    return jnp.roll(spatial, (SHIFT, SHIFT), axis=(1, 2))

def allowed_pairs(region_ids):
    blocks = SIDE // WIN
    window_grid = region_ids.reshape(blocks, WIN, blocks, WIN).transpose(0, 2, 1, 3).reshape(blocks * blocks, WIN * WIN)
    return window_grid[:, :, None] == window_grid[:, None, :]

def offset_grid():
    spots = jnp.arange(WIN * WIN, dtype=jnp.int32)
    rows_at = spots // WIN
    cols_at = spots % WIN
    return (rows_at[:, None] - rows_at[None, :] + WIN - 1) * (2 * WIN - 1) + (cols_at[:, None] - cols_at[None, :] + WIN - 1)

def unpack_matrices(flat_weights):
    bound_one = 3 * D * D
    bound_two = bound_one + D * D
    bound_three = bound_two + D * FF
    return (flat_weights[:bound_one].reshape(D, 3 * D), flat_weights[bound_one:bound_two].reshape(D, D), flat_weights[bound_two:bound_three].reshape(D, FF), flat_weights[bound_three:].reshape(FF, D))

def unpack_small(small):
    pieces = [small[number * D:(number + 1) * D] for number in range(8)]
    bias_up = small[8 * D:8 * D + FF]
    rel_table = small[8 * D + FF:].reshape(REL, HEADS)
    return pieces + [bias_up, rel_table]

def adam_step(weights, first_moment, second_moment, gradient, rate, decay):
    new_first = beta_one * first_moment + (1.0 - beta_one) * gradient
    new_second = beta_two * second_moment + (1.0 - beta_two) * gradient * gradient
    first_hat = new_first / (1.0 - beta_one ** STEP)
    second_hat = new_second / (1.0 - beta_two ** STEP)
    update = first_hat / (jnp.sqrt(second_hat) + adam_eps) + decay * weights
    return (weights - rate * update, new_first, new_second)

def layer_pass(images, cotangent, weights_low, small_parts, allowed, rel_bias):
    weight_qkv, weight_proj, weight_up, weight_down = weights_low
    gain_one, gain_two, shift_one, bias_query, bias_value, bias_proj, shift_two, bias_down, bias_up = small_parts[:9]
    image_count = images.shape[0]
    row_count = image_count * SIDE * SIDE
    places = WIN * WIN
    windows_count = (SIDE // WIN) ** 2
    score_scale = HEAD_DIM ** (-0.5)
    image_values = images.astype(jnp.float32)
    normed_one, scaling_one = norm_stats(image_values)
    input_one = (normed_one * gain_one + shift_one).astype(jnp.bfloat16)
    window_rows = to_windows(input_one).reshape(row_count, D)
    zeros_key = jnp.zeros((D,), jnp.float32)
    projected = jnp.dot(window_rows, weight_qkv, preferred_element_type=jnp.float32) + jnp.concatenate([bias_query, zeros_key, bias_value])
    projected = rounded(projected).reshape(image_count, windows_count, places, 3, HEADS, HEAD_DIM).astype(jnp.float32)
    queries = projected[:, :, :, 0]
    keys_part = projected[:, :, :, 1]
    values_part = projected[:, :, :, 2]
    scores = score_scale * jnp.einsum('bnqhe,bnkhe->bnhqk', queries, keys_part, precision=highest) + rel_bias
    masked = jnp.where(allowed, scores, masked_score)
    row_max = lax.optimization_barrier(jnp.max(masked, axis=-1, keepdims=True))
    log_total = row_max + jnp.log(lax.optimization_barrier(jnp.sum(jnp.exp(masked - row_max), axis=-1, keepdims=True)))
    attention = jnp.exp(masked - log_total)
    attention_low = rounded(attention).astype(jnp.float32)
    mixed_rows = jnp.einsum('bnhqk,bnkhe->bnqhe', attention_low, values_part, precision=highest).astype(jnp.bfloat16).reshape(row_count, D)
    attended = jnp.dot(mixed_rows, weight_proj, preferred_element_type=jnp.float32) + bias_proj
    resid_one = image_values + from_windows(attended.reshape(image_count, windows_count, places, D))
    normed_two, scaling_two = norm_stats(resid_one)
    input_two = (normed_two * gain_two + shift_two).astype(jnp.bfloat16).reshape(row_count, D)
    hidden_pre = jnp.dot(input_two, weight_up, preferred_element_type=jnp.float32) + bias_up
    hidden_act = jax.nn.gelu(hidden_pre, approximate=False).astype(jnp.bfloat16)
    result = resid_one + (jnp.dot(hidden_act, weight_down, preferred_element_type=jnp.float32) + bias_down).reshape(image_count, SIDE, SIDE, D)
    output = result.astype(jnp.bfloat16)
    cot_rows = cotangent.reshape(row_count, D)
    grad_act = jnp.dot(cot_rows, weight_down.T, preferred_element_type=jnp.float32)
    down_grad = jnp.dot(hidden_act.T, cot_rows, preferred_element_type=jnp.float32)
    grad_pre = grad_act * gelu_slope(hidden_pre)
    pre_low = grad_pre.astype(jnp.bfloat16)
    up_grad = jnp.dot(input_two.T, pre_low, preferred_element_type=jnp.float32)
    grad_two = jnp.dot(pre_low, weight_up.T, preferred_element_type=jnp.float32).reshape(image_count, SIDE, SIDE, D)
    second_back, second_gain, second_shift = norm_back(grad_two, normed_two, scaling_two, gain_two)
    grad_resid = cotangent.astype(jnp.float32) + second_back
    grad_rows = to_windows(grad_resid.astype(jnp.bfloat16)).reshape(row_count, D)
    proj_grad = jnp.dot(mixed_rows.T, grad_rows, preferred_element_type=jnp.float32)
    mixed_grad = rounded(jnp.dot(grad_rows, weight_proj.T, preferred_element_type=jnp.float32))
    mixed_grad = mixed_grad.astype(jnp.float32).reshape(image_count, windows_count, places, HEADS, HEAD_DIM)
    value_grad = jnp.einsum('bnhqk,bnqhe->bnkhe', attention_low, mixed_grad, precision=highest)
    prob_grad = jnp.einsum('bnqhe,bnkhe->bnhqk', mixed_grad, values_part, precision=highest)
    row_dot = lax.optimization_barrier(jnp.sum(attention * prob_grad, axis=-1, keepdims=True))
    score_grad = attention * (prob_grad - row_dot)
    score_low = rounded(score_grad).astype(jnp.float32)
    query_grad = score_scale * jnp.einsum('bnhqk,bnkhe->bnqhe', score_low, keys_part, precision=highest)
    key_grad = score_scale * jnp.einsum('bnhqk,bnqhe->bnkhe', score_low, queries, precision=highest)
    qkv_rows = jnp.stack([query_grad, key_grad, value_grad], axis=3).astype(jnp.bfloat16).reshape(row_count, 3 * D)
    qkv_grad = jnp.dot(window_rows.T, qkv_rows, preferred_element_type=jnp.float32)
    grad_one = from_windows(jnp.dot(qkv_rows, weight_qkv.T, preferred_element_type=jnp.float32).reshape(image_count, windows_count, places, D))
    first_back, first_gain, first_shift = norm_back(grad_one, normed_one, scaling_one, gain_one)
    input_grad = (grad_resid + first_back).astype(jnp.bfloat16)
    matrix_part = jnp.concatenate([qkv_grad.reshape(-1), proj_grad.reshape(-1), up_grad.reshape(-1), down_grad.reshape(-1)])
    vector_part = jnp.concatenate([first_gain, second_gain, first_shift, lax.optimization_barrier(jnp.sum(query_grad, axis=(0, 1, 2))).reshape(D), lax.optimization_barrier(jnp.sum(value_grad, axis=(0, 1, 2))).reshape(D), lax.optimization_barrier(jnp.sum(grad_resid, axis=(0, 1, 2))), second_shift, lax.optimization_barrier(jnp.sum(cot_rows.astype(jnp.float32), axis=0)), lax.optimization_barrier(jnp.sum(grad_pre, axis=0))])
    rel_grad = lax.optimization_barrier(jnp.sum(score_grad, axis=(0, 1)))
    return (output, input_grad, matrix_part, vector_part, rel_grad)

def reference(images, cotangent, region_ids, rel_index, matrices, matrix_m, matrix_v, small, small_m, small_v):
    weights_low = unpack_matrices(matrices.astype(jnp.bfloat16))
    small_parts = unpack_small(small)
    allowed = allowed_pairs(region_ids)[None, :, None]
    table_rows = rel_index[offset_grid()]
    rel_bias = small_parts[9][table_rows].transpose(2, 0, 1)
    group_images = IMAGES // N_REP
    image_blocks = images.reshape(N_REP, group_images, SIDE, SIDE, D)
    cot_blocks = cotangent.reshape(N_REP, group_images, SIDE, SIDE, D)

    def advance(running, pair_block):
        output, input_grad, matrix_part, vector_part, rel_grad = layer_pass(pair_block[0], pair_block[1], weights_low, small_parts, allowed, rel_bias)
        return ((running[0] + matrix_part, running[1] + vector_part, running[2] + rel_grad), (output, input_grad))
    initial = (jnp.zeros((MAT,), jnp.float32), jnp.zeros((8 * D + FF,), jnp.float32), jnp.zeros((HEADS, WIN * WIN, WIN * WIN), jnp.float32))
    totals, stacked = lax.scan(advance, initial, (image_blocks, cot_blocks))
    rel_flat = totals[2].transpose(1, 2, 0).reshape(-1, HEADS)
    table_grad = jnp.zeros((REL, HEADS), jnp.float32).at[table_rows.reshape(-1)].add(rel_flat)
    grad_scale = 1.0 / math.sqrt(TOKENS)
    matrix_grad = totals[0] * grad_scale
    small_grad = jnp.concatenate([totals[1], table_grad.reshape(-1)]) * grad_scale
    new_matrices, new_matrix_m, new_matrix_v = adam_step(matrices, matrix_m, matrix_v, matrix_grad, rate_matrix, decay_rate)
    new_small, new_small_m, new_small_v = adam_step(small, small_m, small_v, small_grad, rate_small, 0.0)
    return (stacked[0].reshape(IMAGES, SIDE, SIDE, D), stacked[1].reshape(IMAGES, SIDE, SIDE, D), matrix_grad, small_grad, new_matrices, new_matrix_m, new_matrix_v, new_small, new_small_m, new_small_v)
```

```python
import math

import jax
import jax.numpy as jnp
import numpy as np
from jax import lax
from jax.experimental import pallas as pl
from jax.experimental.pallas import tpu as pltpu
from jax.sharding import PartitionSpec as P

D = 512
HEADS = 16
FF = 2048
WIN = 7
SIDE = 14
SHIFT = 3
STEP = 5
HEAD_DIM = 32
REL = 169

norm_eps = 1e-05
beta_one = 0.9
beta_two = 0.999
adam_eps = 1e-08
rate_matrix = 0.01
rate_small = 0.2
decay_rate = 0.05
masked_score = -1e30
root_half = 0.7071067811865476
inv_root_twopi = 0.3989422804014327
highest = lax.Precision.HIGHEST
score_scale = HEAD_DIM ** (-0.5)

PLACES = WIN * WIN
PAD = 64
WINDOWS = (SIDE // WIN) ** 2
ROWS = WINDOWS * PAD
STRIP = 16
FLAT = SIDE * STRIP
GROUP = 4
GROUPS = HEADS // GROUP
LANES = GROUP * HEAD_DIM
WIDE = GROUP * PAD

PIECE = 64
UP_ROWS = PIECE // (FF // D)
BLOCKS = (3 * D * D + D * D + 2 * D * FF) // (PIECE * D)
QKV_END = 3 * D // PIECE
PROJ_END = QKV_END + D // PIECE
UP_END = PROJ_END + FF // PIECE
KINDS = 4 + 2 * (FF // D)
SMALL_ROWS = 8 + FF // D
f32 = jnp.float32
bf16 = jnp.bfloat16


def window_source():
    source = np.full((ROWS,), -1, np.int64)
    blocks = SIDE // WIN
    for window in range(WINDOWS):
        for place in range(PLACES):
            row = (window // blocks * WIN + place // WIN + SHIFT) % SIDE
            col = (window % blocks * WIN + place % WIN + SHIFT) % SIDE
            source[window * PAD + place] = row * STRIP + col
    return source


def permutation():
    return (window_source()[:, None] == np.arange(FLAT)[None, :]).astype(np.float32)


def dot(a, b):
    return lax.dot_general(a, b, (((1,), (0,)), ((), ())), preferred_element_type=f32)


def dot_t(a, b):
    return lax.dot_general(a, b, (((1,), (1,)), ((), ())), preferred_element_type=f32)


def t_dot(a, b):
    return lax.dot_general(a, b, (((0,), (0,)), ((), ())), preferred_element_type=f32)


def norm_stats(values):
    center = values - jnp.mean(values, axis=-1, keepdims=True)
    spread = jnp.mean(center * center, axis=-1, keepdims=True)
    scaling = lax.rsqrt(spread + norm_eps)
    return center * scaling, scaling


def norm_back(incoming, normed, scaling, gain_vector):
    scaled = incoming * gain_vector
    return scaling * (
        scaled
        - jnp.mean(scaled, axis=-1, keepdims=True)
        - normed * jnp.mean(scaled * normed, axis=-1, keepdims=True)
    )


def col_sum(values):
    return jnp.sum(values, axis=0, keepdims=True)


def layer_kernel(counts, out_counts):
    n_in = len(counts)
    n_out = len(out_counts)

    def body(*refs):
        slots, out_slots = refs[0], refs[1]
        img, cot, perm, small, bias, reg_key, reg_query = refs[2:9]
        pieces = refs[9 : 9 + n_in]
        refs = refs[9 + n_in :]
        out, in_grad, sums, rel_sum = refs[:4]
        grads = refs[4 : 4 + n_out]
        (
            weights,
            wgrad,
            flat,
            xw,
            cw,
            in_one,
            qkv,
            att,
            att_low,
            mixed,
            resid,
            in_two,
            act,
            acc,
            acc_two,
            pre,
            gres,
            grow,
            mgrad,
            dqkv,
            ext,
            sem,
            sem_out,
        ) = refs[4 + n_out :]

        def place(third, make, make_up):
            @pl.when(third < QKV_END)
            def _():
                make(lax.rem(third, 3), lax.div(third, 3) * PIECE)

            @pl.when((third >= QKV_END) & (third < PROJ_END))
            def _():
                make(3, (third - QKV_END) * PIECE)

            @pl.when((third >= PROJ_END) & (third < UP_END))
            def _():
                make_up((third - PROJ_END) * UP_ROWS)

            @pl.when(third >= UP_END)
            def _():
                at = third - UP_END
                make(4 + FF // D + lax.div(at, D // PIECE), lax.rem(at, D // PIECE) * PIECE)

        base = 0
        for number, count in enumerate(counts):

            def fetch(slot, carry, number=number, base=base):
                source = pieces[number].at[slot]

                def make(block, row):
                    row = pl.multiple_of(row, PIECE)
                    pltpu.make_async_copy(source, weights.at[block, pl.ds(row, PIECE)], sem).start()

                def make_up(row):
                    row = pl.multiple_of(row, UP_ROWS)
                    for j in range(FF // D):
                        pltpu.make_async_copy(
                            source.at[pl.ds(j * UP_ROWS, UP_ROWS)],
                            weights.at[4 + j, pl.ds(row, UP_ROWS)],
                            sem,
                        ).start()

                place(slots[base + slot], make, make_up)
                return carry

            lax.fori_loop(0, count, fetch, 0)
            base += count

        gain_one, gain_two, shift_one, bias_query, bias_value, bias_proj, shift_two, bias_down = (
            small[number : number + 1, :] for number in range(8)
        )

        flat[...] = jnp.zeros_like(flat)
        for row in range(SIDE):
            flat[row * STRIP : row * STRIP + SIDE, :] = img[0, row]
        xw[...] = dot(perm[...], flat[...])
        for row in range(SIDE):
            flat[row * STRIP : row * STRIP + SIDE, :] = cot[0, row]
        cw[...] = dot(perm[...], flat[...]).astype(bf16)

        def rows_of(number, size):
            return pl.ds(pl.multiple_of(number * size, size), size)

        def norm_one(number, carry):
            at = rows_of(number, PAD)
            normed, _ = norm_stats(xw[at, :])
            in_one[at, :] = (normed * gain_one + shift_one).astype(bf16)
            return carry

        lax.fori_loop(0, WINDOWS, norm_one, 0)

        for window in range(WINDOWS):
            allowed = reg_key[window] == reg_query[window]
            for group in range(GROUPS):
                ext[window, group] = jnp.where(
                    allowed, bias[:, group * WIDE : (group + 1) * WIDE], masked_score
                )
        head_mask = (
            lax.broadcasted_iota(jnp.int32, (WIDE, LANES), 0) // PAD
            == lax.broadcasted_iota(jnp.int32, (WIDE, LANES), 1) // HEAD_DIM
        )

        def spread_heads(values):
            return jnp.where(head_mask, jnp.concatenate([values] * GROUP, axis=0), 0)

        def join_heads(values):
            kept = jnp.where(head_mask, values, 0.0)
            total = kept[:PAD]
            for head in range(1, GROUP):
                total = total + kept[head * PAD : (head + 1) * PAD]
            return total

        pltpu.make_async_copy(weights, weights, sem).wait()

        for part, vector in enumerate((bias_query, None, bias_value)):
            product = dot(in_one[...], weights[part])
            if vector is not None:
                product = product + vector
            qkv[part] = product.astype(bf16)

        def attend(window, carry):
            at = rows_of(window, PAD)
            for group in range(GROUPS):
                lanes = slice(group * LANES, (group + 1) * LANES)
                scores = dot_t(qkv[1, at, lanes], spread_heads(qkv[0, at, lanes]))
                masked = score_scale * scores + ext[window, group]
                top = jnp.max(masked, axis=0, keepdims=True)
                raised = jnp.exp(masked - top)
                attention = raised * (1.0 / col_sum(raised))
                low = attention.astype(bf16)
                att[window, group] = attention
                att_low[window, group] = low
                mixed[at, lanes] = join_heads(t_dot(low, qkv[2, at, lanes])).astype(bf16)
            return carry

        lax.fori_loop(0, WINDOWS, attend, 0)

        resid[...] = xw[...] + (dot(mixed[...], weights[3]) + bias_proj)

        def norm_two(number, carry):
            at = rows_of(number, PAD)
            normed, _ = norm_stats(resid[at, :])
            in_two[at, :] = (normed * gain_two + shift_two).astype(bf16)
            return carry

        lax.fori_loop(0, WINDOWS, norm_two, 0)

        def feed(j, carry):
            up = weights.at[4 + j]
            down = weights.at[4 + FF // D + j]
            acc_two[...] = dot(in_two[...], up[...]) + small[pl.ds(8 + j, 1), :]
            pre[...] = dot_t(cw[...], down[...])

            def gelu_part(number, total):
                at = rows_of(number, 32)
                value = acc_two[at, :]
                phi = 0.5 * (1.0 + lax.erf(value * root_half))
                act[at, :] = (value * phi).astype(bf16)
                slope = phi + value * jnp.exp(-0.5 * value * value) * inv_root_twopi
                back = pre[at, :] * slope
                grow[at, :] = back.astype(bf16)
                return total + col_sum(back)

            sums[pl.ds(8 + j, 1), :] = lax.fori_loop(
                0, ROWS // 32, gelu_part, jnp.zeros((1, D), f32)
            )
            forward = dot(act[...], down[...])
            backward = dot_t(grow[...], up[...])

            @pl.when(j == 0)
            def _():
                acc[...] = forward
                gres[...] = backward

            @pl.when(j > 0)
            def _():
                acc[...] += forward
                gres[...] += backward

            wgrad[4 + j] = t_dot(in_two[...], grow[...]).astype(bf16)
            wgrad[4 + FF // D + j] = t_dot(act[...], cw[...]).astype(bf16)
            return carry

        lax.fori_loop(0, FF // D, feed, 0)

        def second_back(number, carry):
            gain_sum, shift_sum, resid_sum, cot_sum = carry
            at = rows_of(number, 32)
            value = resid[at, :]
            normed, scaling = norm_stats(value)
            act[at, :] = (value + (acc[at, :] + bias_down)).astype(bf16)
            incoming = gres[at, :]
            back = norm_back(incoming, normed, scaling, gain_two)
            cotangent = cw[at, :].astype(f32)
            total = cotangent + back
            gres[at, :] = total
            grow[at, :] = total.astype(bf16)
            return (
                gain_sum + col_sum(incoming * normed),
                shift_sum + col_sum(incoming),
                resid_sum + col_sum(total),
                cot_sum + col_sum(cotangent),
            )

        zero_row = jnp.zeros((1, D), f32)
        sums[1:2, :], sums[6:7, :], sums[5:6, :], sums[7:8, :] = lax.fori_loop(
            0, ROWS // 32, second_back, (zero_row,) * 4
        )
        result = t_dot(perm[...], act[...]).astype(bf16)
        for row in range(SIDE):
            out[0, row] = result[row * STRIP : row * STRIP + SIDE, :]

        wgrad[3] = t_dot(mixed[...], grow[...]).astype(bf16)
        mgrad[...] = dot_t(grow[...], weights[3]).astype(bf16)
        sums[3:4, :] = zero_row
        sums[4:5, :] = zero_row
        rel_sum[...] = jnp.zeros_like(rel_sum)

        def attend_back(window, carry):
            at = rows_of(window, PAD)
            for group in range(GROUPS):
                lanes = slice(group * LANES, (group + 1) * LANES)
                wide = slice(group * WIDE, (group + 1) * WIDE)
                mixed_blk = spread_heads(mgrad[at, lanes])
                query_blk = spread_heads(qkv[0, at, lanes])
                prob = dot_t(qkv[2, at, lanes], mixed_blk)
                attention = att[window, group]
                score = attention * (prob - col_sum(attention * prob))
                rel_sum[:, wide] += score
                low = score.astype(bf16)
                value_grad = dot(att_low[window, group], mixed_blk)
                key_grad = score_scale * dot(low, query_blk)
                query_grad = score_scale * join_heads(t_dot(low, qkv[1, at, lanes]))
                sums[3:4, lanes] += col_sum(query_grad)
                sums[4:5, lanes] += col_sum(value_grad)
                dqkv[0, at, lanes] = query_grad.astype(bf16)
                dqkv[1, at, lanes] = key_grad.astype(bf16)
                dqkv[2, at, lanes] = value_grad.astype(bf16)
            return carry

        lax.fori_loop(0, WINDOWS, attend_back, 0)

        for part in range(3):
            wgrad[part] = t_dot(in_one[...], dqkv[part]).astype(bf16)

        base = 0
        for number, count in enumerate(out_counts):

            def store(slot, carry, number=number, base=base):
                target = grads[number].at[slot]

                def make(block, row):
                    row = pl.multiple_of(row, PIECE)
                    pltpu.make_async_copy(
                        wgrad.at[block, pl.ds(row, PIECE)], target, sem_out
                    ).start()

                def make_up(row):
                    row = pl.multiple_of(row, UP_ROWS)
                    for j in range(FF // D):
                        pltpu.make_async_copy(
                            wgrad.at[4 + j, pl.ds(row, UP_ROWS)],
                            target.at[pl.ds(j * UP_ROWS, UP_ROWS)],
                            sem_out,
                        ).start()

                place(out_slots[base + slot], make, make_up)
                return carry

            lax.fori_loop(0, count, store, 0)
            base += count

        acc[...] = dot_t(dqkv[0], weights[0])
        acc[...] += dot_t(dqkv[1], weights[1])
        acc[...] += dot_t(dqkv[2], weights[2])

        def first_back(number, carry):
            gain_sum, shift_sum = carry
            at = rows_of(number, 32)
            normed, scaling = norm_stats(xw[at, :])
            incoming = acc[at, :]
            back = norm_back(incoming, normed, scaling, gain_one)
            act[at, :] = (gres[at, :] + back).astype(bf16)
            return gain_sum + col_sum(incoming * normed), shift_sum + col_sum(incoming)

        sums[0:1, :], sums[2:3, :] = lax.fori_loop(0, ROWS // 32, first_back, (zero_row,) * 2)
        result = t_dot(perm[...], act[...]).astype(bf16)
        for row in range(SIDE):
            in_grad[0, row] = result[row * STRIP : row * STRIP + SIDE, :]
        pltpu.make_async_copy(wgrad, wgrad, sem_out).wait()

    return body


def run_layer(images, cotangent, small, bias, reg_key, reg_query, pieces, slots, out_slots, outs):
    perm = jnp.asarray(permutation(), bf16)
    vmem = pl.BlockSpec(memory_space=pltpu.VMEM)
    smem = pl.BlockSpec(memory_space=pltpu.SMEM)
    hbm = pl.BlockSpec(memory_space=pl.ANY)
    counts = [piece.shape[0] for piece in pieces]
    image_shape = (1, SIDE, SIDE, D)
    return pl.pallas_call(
        layer_kernel(counts, outs),
        in_specs=[smem, smem] + [vmem] * 7 + [hbm] * len(counts),
        out_specs=[vmem] * 4 + [hbm] * len(outs),
        out_shape=[
            jax.ShapeDtypeStruct(image_shape, bf16),
            jax.ShapeDtypeStruct(image_shape, bf16),
            jax.ShapeDtypeStruct((SMALL_ROWS, D), f32),
            jax.ShapeDtypeStruct((PAD, HEADS * PAD), f32),
        ]
        + [jax.ShapeDtypeStruct((count, PIECE, D), bf16) for count in outs],
        scratch_shapes=[
            pltpu.VMEM((KINDS, D, D), bf16),
            pltpu.VMEM((KINDS, D, D), bf16),
            pltpu.VMEM((FLAT, D), bf16),
            pltpu.VMEM((ROWS, D), f32),
            pltpu.VMEM((ROWS, D), bf16),
            pltpu.VMEM((ROWS, D), bf16),
            pltpu.VMEM((3, ROWS, D), bf16),
            pltpu.VMEM((WINDOWS, GROUPS, PAD, WIDE), f32),
            pltpu.VMEM((WINDOWS, GROUPS, PAD, WIDE), bf16),
            pltpu.VMEM((ROWS, D), bf16),
            pltpu.VMEM((ROWS, D), f32),
            pltpu.VMEM((ROWS, D), bf16),
            pltpu.VMEM((ROWS, D), bf16),
            pltpu.VMEM((ROWS, D), f32),
            pltpu.VMEM((ROWS, D), f32),
            pltpu.VMEM((ROWS, D), f32),
            pltpu.VMEM((ROWS, D), f32),
            pltpu.VMEM((ROWS, D), bf16),
            pltpu.VMEM((ROWS, D), bf16),
            pltpu.VMEM((3, ROWS, D), bf16),
            pltpu.VMEM((WINDOWS, GROUPS, PAD, WIDE), f32),
            pltpu.SemaphoreType.DMA,
            pltpu.SemaphoreType.DMA,
        ],
        name="layer",
    )(slots, out_slots, images, cotangent, perm, small, bias, reg_key, reg_query, *pieces)


VIEW = PIECE * D * 3 // 128


def shard_kinds(device):
    third = 3 * device + jnp.arange(3, dtype=jnp.int32)
    is_up = (third >= PROJ_END) & (third < UP_END)
    return jnp.where(third < QKV_END, 0, jnp.where(is_up, 2, 1)).astype(jnp.int32)


def piece_rows(kind, part):
    per_row = D // 128
    if kind == 0:
        return [(slice(0, PIECE), per_row * part, 3 * per_row)]
    if kind == 1:
        return [(slice(0, PIECE), per_row * PIECE * part, per_row)]
    return [
        (slice(j * UP_ROWS, (j + 1) * UP_ROWS), per_row * (PIECE * part + j), per_row * (FF // D))
        for j in range(FF // D)
    ]


def pack_kernel(kinds, shard, *outs):
    for part in range(3):
        for kind in range(3):

            @pl.when(kinds[part] == kind)
            def _(part=part, kind=kind):
                for rows, start, stride in piece_rows(kind, part):
                    size = rows.stop - rows.start
                    for lane in range(D // 128):
                        outs[part][0, rows, lane * 128 : (lane + 1) * 128] = shard[
                            pl.ds(start + lane, size, stride=stride), :
                        ].astype(bf16)


def pack_shard(shard, kinds):
    vmem = pl.BlockSpec(memory_space=pltpu.VMEM)
    return pl.pallas_call(
        pack_kernel,
        in_specs=[pl.BlockSpec(memory_space=pltpu.SMEM), vmem],
        out_specs=[vmem] * 3,
        out_shape=[jax.ShapeDtypeStruct((1, PIECE, D), bf16)] * 3,
        name="pack",
    )(kinds, shard.reshape(VIEW, 128))


def adam_step(weights, first_moment, second_moment, gradient, rate, decay):
    new_first = beta_one * first_moment + (1.0 - beta_one) * gradient
    new_second = beta_two * second_moment + (1.0 - beta_two) * gradient * gradient
    first_hat = new_first / (1.0 - beta_one**STEP)
    second_hat = new_second / (1.0 - beta_two**STEP)
    update = first_hat / (jnp.sqrt(second_hat) + adam_eps) + decay * weights
    return (weights - rate * update, new_first, new_second)


def adam_kernel(grad_scale):
    def body(kinds, *refs):
        parts = refs[:6]
        weights, first, second = refs[6:9]
        grad, new_weights, new_first, new_second = refs[9:13]
        for part in range(3):
            for kind in range(3):

                @pl.when(kinds[part] == kind)
                def _(part=part, kind=kind):
                    for rows, start, stride in piece_rows(kind, part):
                        size = rows.stop - rows.start
                        for lane in range(D // 128):
                            lanes = slice(lane * 128, (lane + 1) * 128)
                            total = parts[2 * part][0, rows, lanes].astype(f32) + parts[
                                2 * part + 1
                            ][0, rows, lanes].astype(f32)
                            grad[pl.ds(start + lane, size, stride=stride), :] = total * grad_scale

        def step(number, carry):
            at = pl.ds(pl.multiple_of(number * 64, 64), 64)
            new_weights[at, :], new_first[at, :], new_second[at, :] = adam_step(
                weights[at, :], first[at, :], second[at, :], grad[at, :], rate_matrix, decay_rate
            )
            return carry

        lax.fori_loop(0, VIEW // 64, step, 0)

    return body


def adam_shard(kinds, parts, weights, first, second, grad_scale):
    vmem = pl.BlockSpec(memory_space=pltpu.VMEM)
    size = weights.shape[0]
    results = pl.pallas_call(
        adam_kernel(grad_scale),
        in_specs=[pl.BlockSpec(memory_space=pltpu.SMEM)] + [vmem] * 9,
        out_specs=[vmem] * 4,
        out_shape=[jax.ShapeDtypeStruct((VIEW, 128), f32)] * 4,
        name="adam",
    )(kinds, *parts, *(array.reshape(VIEW, 128) for array in (weights, first, second)))
    return [result.reshape(size) for result in results]


def to_pieces(flat):
    q_end, p_end, u_end = QKV_END * PIECE * D, PROJ_END * PIECE * D, UP_END * PIECE * D
    qkv = flat[:q_end].reshape(-1, PIECE, 3, D).transpose(0, 2, 1, 3).reshape(-1, PIECE, D)
    proj = flat[q_end:p_end].reshape(-1, PIECE, D)
    up = flat[p_end:u_end].reshape(-1, UP_ROWS, FF // D, D).transpose(0, 2, 1, 3)
    down = flat[u_end:].reshape(-1, PIECE, D)
    return jnp.concatenate([qkv, proj, up.reshape(-1, PIECE, D), down])


def from_pieces(pieces):
    qkv = pieces[:QKV_END].reshape(-1, 3, PIECE, D).transpose(0, 2, 1, 3)
    up = pieces[PROJ_END:UP_END].reshape(-1, FF // D, UP_ROWS, D).transpose(0, 2, 1, 3)
    return jnp.concatenate(
        [
            qkv.reshape(-1),
            pieces[QKV_END:PROJ_END].reshape(-1),
            up.reshape(-1),
            pieces[UP_END:].reshape(-1),
        ]
    )


def offset_grid():
    spots = np.arange(PAD)
    rows_at = spots // WIN
    cols_at = spots % WIN
    grid = (rows_at[None, :] - rows_at[:, None] + WIN - 1) * (2 * WIN - 1) + (
        cols_at[None, :] - cols_at[:, None] + WIN - 1
    )
    real = (spots[:, None] < PLACES) & (spots[None, :] < PLACES)
    return np.where(real, grid, -1)


AXES = ("rep", "grp")


def on_device(
    images, cotangent, region_ids, rel_index, matrices, matrix_m, matrix_v, small, small_m, small_v
):
    devices = lax.axis_size("rep") * lax.axis_size("grp")
    me = lax.axis_index(AXES)
    bits = [1 << number for number in range(devices.bit_length() - 1)]
    exact = devices == sum(bits) + 1 and matrices.shape[0] == 3 * PIECE * D

    def swap(value, bit):
        return lax.ppermute(value, AXES, [(i, i ^ bit) for i in range(devices)])

    small_rows = small[: SMALL_ROWS * D].reshape(SMALL_ROWS, D)
    rel_table = small[SMALL_ROWS * D :].reshape(REL, HEADS)

    if exact:
        core, y_bit, x_bit = bits[0], bits[1], bits[2]
        z_bits = bits[3:]
        orders = [
            [x_bit, y_bit] + z_bits,
            [y_bit] + z_bits[:1] + [x_bit] + z_bits[1:],
            z_bits[:1] + [x_bit, y_bit] + z_bits[1:],
        ]
        kinds = shard_kinds(me)
        packed = pack_shard(matrices, kinds)
        pieces = []
        piece_slots = []
        for color in range(3):
            buffer = packed[color]
            masks = [0]
            for bit in reversed(orders[color][1:]):
                buffer = jnp.concatenate([buffer, swap(buffer, bit)])
                masks = masks + [mask ^ bit for mask in masks]
            last = orders[color][0]
            far = swap(buffer, last)
            for value, extra in (
                (buffer, 0),
                (far, last),
                (swap(buffer, core), core),
                (swap(far, core), last ^ core),
            ):
                pieces.append(value)
                piece_slots += [(mask ^ extra, color) for mask in masks]
        masks = jnp.asarray([mask for mask, _ in piece_slots], jnp.int32)
        colors = jnp.asarray([color for _, color in piece_slots], jnp.int32)
        slots = 3 * (me ^ masks) + colors
        out_pieces = []
        for color in range(3):
            order = orders[color]
            half = [0]
            for bit in reversed(order[1:]):
                half = half + [mask ^ bit for mask in half]
            for extra in (order[0] ^ core, core, order[0], 0):
                out_pieces += [(mask ^ extra, color) for mask in half]
        out_slots = 3 * (me ^ jnp.asarray([m for m, _ in out_pieces], jnp.int32)) + jnp.asarray(
            [c for _, c in out_pieces], jnp.int32
        )
        outs = [devices // 4] * 12
    else:
        gathered = lax.all_gather(matrices.astype(bf16), AXES, axis=0, tiled=True)
        pieces = [to_pieces(gathered)]
        slots = jnp.arange(BLOCKS, dtype=jnp.int32)
        out_slots = slots
        outs = [BLOCKS]

    labels = jnp.arange(REL, dtype=jnp.int32)
    grid = jnp.asarray(offset_grid(), jnp.int32)
    select_offset = (grid[None] == labels[:, None, None]).astype(f32)
    select_row = (rel_index[:, None] == labels[None, :]).astype(f32)
    table_rows = jnp.dot(select_row, rel_table, precision=highest)
    bias = jnp.einsum("okq,oh->khq", select_offset, table_rows, precision=highest)
    bias = bias.reshape(PAD, HEADS * PAD)
    blocks = SIDE // WIN
    regions = (
        region_ids.reshape(blocks, WIN, blocks, WIN).transpose(0, 2, 1, 3).reshape(WINDOWS, PLACES)
    )
    padded = ((0, 0), (0, PAD - PLACES))
    reg_key = jnp.pad(regions, padded, constant_values=-1)[:, :, None]
    reg_query = jnp.tile(jnp.pad(regions, padded, constant_values=-2), (1, GROUP))[:, None, :]

    output, input_grad, sums, rel_sum, *grads = run_layer(
        images, cotangent, small_rows, bias, reg_key, reg_query, pieces, slots, out_slots, outs
    )

    tokens_all = images.shape[0] * devices * SIDE * SIDE
    grad_scale = 1.0 / math.sqrt(tokens_all)
    rel_grad = jnp.einsum(
        "okq,khq->oh", select_offset, rel_sum.reshape(PAD, HEADS, PAD), precision=highest
    )
    table_grad = jnp.dot(select_row.T, rel_grad, precision=highest)
    small_local = jnp.concatenate([sums.reshape(-1), table_grad.reshape(-1)]) * grad_scale

    if exact:
        parts = []
        for color in range(3):
            order = orders[color]
            send_far, send_near, keep_far, keep_near = grads[4 * color : 4 * color + 4]

            def add(a, b):
                return (a.astype(f32) + b.astype(f32)).astype(bf16)

            far = add(keep_far, swap(send_far, core))
            near = add(keep_near, swap(send_near, core))
            for number, bit in enumerate(order):
                received = swap(far, bit)
                if number == len(order) - 1:
                    parts += [near, received]
                    break
                size = near.shape[0] // 2
                far = add(near[size:], received[size:])
                near = add(near[:size], received[:size])
        owned_grad, new_matrices, new_matrix_m, new_matrix_v = adam_shard(
            kinds, parts, matrices, matrix_m, matrix_v, grad_scale
        )
        small_grad = small_local
        for bit in bits:
            small_grad = small_grad + swap(small_grad, bit)
    else:
        flat_grad = from_pieces(grads[0].astype(f32)) * grad_scale
        owned_grad = lax.psum_scatter(flat_grad, AXES, scatter_dimension=0, tiled=True)
        new_matrices, new_matrix_m, new_matrix_v = adam_step(
            matrices, matrix_m, matrix_v, owned_grad, rate_matrix, decay_rate
        )
        small_grad = lax.psum(small_local, AXES)
    new_small, new_small_m, new_small_v = adam_step(
        small, small_m, small_v, small_grad, rate_small, 0.0
    )
    return (
        output,
        input_grad,
        owned_grad,
        small_grad,
        new_matrices,
        new_matrix_m,
        new_matrix_v,
        new_small,
        new_small_m,
        new_small_v,
    )


def solution(mesh):
    tokens = P(AXES, None, None, None)
    shard = P(AXES)
    whole = P()
    return jax.shard_map(
        on_device,
        mesh=mesh,
        in_specs=(tokens, tokens, whole, whole, shard, shard, shard, whole, whole, whole),
        out_specs=(tokens, tokens, shard, whole, shard, shard, shard, whole, whole, whole),
        check_vma=False,
    )
```

```python
import math

import jax
import jax.numpy as jnp
import numpy as np
from jax import lax
from jax.experimental import pallas as pl
from jax.experimental.pallas import tpu as pltpu
from jax.sharding import PartitionSpec as P


D = 512
HEADS = 16
FF = 2048
WIN = 7
SIDE = 14
SHIFT = 3
STEP = 5
HEAD_DIM = 32
REL = 169

norm_eps = 1e-05
beta_one = 0.9
beta_two = 0.999
adam_eps = 1e-08
rate_matrix = 0.01
rate_small = 0.2
decay_rate = 0.05
masked_score = -1e30
root_half = 0.7071067811865476
inv_root_twopi = 0.3989422804014327
highest = lax.Precision.HIGHEST
score_scale = HEAD_DIM ** (-0.5)

PLACES = WIN * WIN
PAD = 64
WINDOWS = (SIDE // WIN) ** 2
ROWS = WINDOWS * PAD
STRIP = 16
FLAT = SIDE * STRIP
GROUP = 4
GROUPS = HEADS // GROUP
LANES = GROUP * HEAD_DIM
WIDE = GROUP * PAD

PIECE = 64
UP_ROWS = PIECE // (FF // D)
BLOCKS = (3 * D * D + D * D + 2 * D * FF) // (PIECE * D)
QKV_END = 3 * D // PIECE
PROJ_END = QKV_END + D // PIECE
UP_END = PROJ_END + FF // PIECE
KINDS = 4 + 2 * (FF // D)
SMALL_ROWS = 8 + FF // D
f32 = jnp.float32
bf16 = jnp.bfloat16


def window_source():
    source = np.full((ROWS,), -1, np.int64)
    blocks = SIDE // WIN
    for window in range(WINDOWS):
        for place in range(PLACES):
            row = (window // blocks * WIN + place // WIN + SHIFT) % SIDE
            col = (window % blocks * WIN + place % WIN + SHIFT) % SIDE
            source[window * PAD + place] = row * STRIP + col
    return source


def permutation():
    return (window_source()[:, None] == np.arange(FLAT)[None, :]).astype(np.float32)


def dot(a, b):
    return lax.dot_general(a, b, (((1,), (0,)), ((), ())), preferred_element_type=f32)


def dot_t(a, b):
    return lax.dot_general(a, b, (((1,), (1,)), ((), ())), preferred_element_type=f32)


def t_dot(a, b):
    return lax.dot_general(a, b, (((0,), (0,)), ((), ())), preferred_element_type=f32)


def norm_stats(values):
    center = values - jnp.mean(values, axis=-1, keepdims=True)
    spread = jnp.mean(center * center, axis=-1, keepdims=True)
    scaling = lax.rsqrt(spread + norm_eps)
    return center * scaling, scaling


def norm_back(incoming, normed, scaling, gain_vector):
    scaled = incoming * gain_vector
    return scaling * (
        scaled
        - jnp.mean(scaled, axis=-1, keepdims=True)
        - normed * jnp.mean(scaled * normed, axis=-1, keepdims=True)
    )


def col_sum(values):
    return jnp.sum(values, axis=0, keepdims=True)


def layer_kernel(counts, out_counts):
    n_in = len(counts)
    n_out = len(out_counts)

    def body(*refs):
        slots, out_slots = refs[0], refs[1]
        img, cot, perm, small, bias, mask = refs[2:8]
        pieces = refs[8 : 8 + n_in]
        refs = refs[8 + n_in :]
        out, in_grad, sums, rel_sum = refs[:4]
        grads = refs[4 : 4 + n_out]
        (
            weights,
            wgrad,
            flat,
            xw,
            cw,
            in_one,
            qkv,
            att,
            att_low,
            mixed,
            resid,
            in_two,
            act,
            acc,
            acc_two,
            pre,
            gres,
            grow,
            mgrad,
            dqkv,
            ext,
            sem,
            sem_out,
        ) = refs[4 + n_out :]

        def place(third, make, make_up):
            @pl.when(third < QKV_END)
            def _():
                make(lax.rem(third, 3), lax.div(third, 3) * PIECE)

            @pl.when((third >= QKV_END) & (third < PROJ_END))
            def _():
                make(3, (third - QKV_END) * PIECE)

            @pl.when((third >= PROJ_END) & (third < UP_END))
            def _():
                make_up((third - PROJ_END) * UP_ROWS)

            @pl.when(third >= UP_END)
            def _():
                at = third - UP_END
                make(4 + FF // D + lax.div(at, D // PIECE), lax.rem(at, D // PIECE) * PIECE)

        base = 0
        for number, count in enumerate(counts):

            def fetch(slot, carry, number=number, base=base):
                source = pieces[number].at[slot]

                def make(block, row):
                    row = pl.multiple_of(row, PIECE)
                    pltpu.make_async_copy(source, weights.at[block, pl.ds(row, PIECE)], sem).start()

                def make_up(row):
                    row = pl.multiple_of(row, UP_ROWS)
                    for j in range(FF // D):
                        pltpu.make_async_copy(
                            source.at[pl.ds(j * UP_ROWS, UP_ROWS)],
                            weights.at[4 + j, pl.ds(row, UP_ROWS)],
                            sem,
                        ).start()

                place(slots[base + slot], make, make_up)
                return carry

            lax.fori_loop(0, count, fetch, 0)
            base += count

        gain_one, gain_two, shift_one, bias_query, bias_value, bias_proj, shift_two, bias_down = (
            small[number : number + 1, :] for number in range(8)
        )

        flat[...] = jnp.zeros_like(flat)
        for row in range(SIDE):
            flat[row * STRIP : row * STRIP + SIDE, :] = img[0, row]
        xw[...] = dot(perm[...], flat[...])
        for row in range(SIDE):
            flat[row * STRIP : row * STRIP + SIDE, :] = cot[0, row]
        cw[...] = dot(perm[...], flat[...]).astype(bf16)

        def rows_of(number, size):
            return pl.ds(pl.multiple_of(number * size, size), size)

        def norm_one(number, carry):
            at = rows_of(number, PAD)
            normed, _ = norm_stats(xw[at, :])
            in_one[at, :] = (normed * gain_one + shift_one).astype(bf16)
            return carry

        lax.fori_loop(0, WINDOWS, norm_one, 0)

        for window in range(WINDOWS):
            allowed = mask[window] != 0
            for group in range(GROUPS):
                ext[window, group] = jnp.where(
                    allowed, bias[:, group * WIDE : (group + 1) * WIDE], masked_score
                )
        head_mask = (
            lax.broadcasted_iota(jnp.int32, (WIDE, LANES), 0) // PAD
            == lax.broadcasted_iota(jnp.int32, (WIDE, LANES), 1) // HEAD_DIM
        )

        def spread_heads(values):
            return jnp.where(head_mask, jnp.concatenate([values] * GROUP, axis=0), 0)

        def join_heads(values):
            kept = jnp.where(head_mask, values, 0.0)
            total = kept[:PAD]
            for head in range(1, GROUP):
                total = total + kept[head * PAD : (head + 1) * PAD]
            return total

        pltpu.make_async_copy(weights, weights, sem).wait()

        for part, vector in enumerate((bias_query, None, bias_value)):
            product = dot(in_one[...], weights[part])
            if vector is not None:
                product = product + vector
            qkv[part] = product.astype(bf16)

        def attend(window, carry):
            at = rows_of(window, PAD)
            for group in range(GROUPS):
                lanes = slice(group * LANES, (group + 1) * LANES)
                scores = dot_t(qkv[1, at, lanes], spread_heads(qkv[0, at, lanes]))
                masked = score_scale * scores + ext[window, group]
                top = jnp.max(masked, axis=0, keepdims=True)
                raised = jnp.exp(masked - top)
                attention = raised * (1.0 / col_sum(raised))
                low = attention.astype(bf16)
                att[window, group] = attention
                att_low[window, group] = low
                mixed[at, lanes] = join_heads(t_dot(low, qkv[2, at, lanes])).astype(bf16)
            return carry

        lax.fori_loop(0, WINDOWS, attend, 0)

        resid[...] = xw[...] + (dot(mixed[...], weights[3]) + bias_proj)

        def norm_two(number, carry):
            at = rows_of(number, PAD)
            normed, _ = norm_stats(resid[at, :])
            in_two[at, :] = (normed * gain_two + shift_two).astype(bf16)
            return carry

        lax.fori_loop(0, WINDOWS, norm_two, 0)

        def feed(j, carry):
            up = weights.at[4 + j]
            down = weights.at[4 + FF // D + j]
            acc_two[...] = dot(in_two[...], up[...]) + small[pl.ds(8 + j, 1), :]
            pre[...] = dot_t(cw[...], down[...])

            def gelu_part(number, total):
                at = rows_of(number, 32)
                value = acc_two[at, :]
                phi = 0.5 * (1.0 + lax.erf(value * root_half))
                act[at, :] = (value * phi).astype(bf16)
                slope = phi + value * jnp.exp(-0.5 * value * value) * inv_root_twopi
                back = pre[at, :] * slope
                grow[at, :] = back.astype(bf16)
                return total + col_sum(back)

            sums[pl.ds(8 + j, 1), :] = lax.fori_loop(
                0, ROWS // 32, gelu_part, jnp.zeros((1, D), f32)
            )
            forward = dot(act[...], down[...])
            backward = dot_t(grow[...], up[...])

            @pl.when(j == 0)
            def _():
                acc[...] = forward
                gres[...] = backward

            @pl.when(j > 0)
            def _():
                acc[...] += forward
                gres[...] += backward

            wgrad[4 + j] = t_dot(in_two[...], grow[...]).astype(bf16)
            wgrad[4 + FF // D + j] = t_dot(act[...], cw[...]).astype(bf16)
            return carry

        lax.fori_loop(0, FF // D, feed, 0)

        def second_back(number, carry):
            gain_sum, shift_sum, resid_sum, cot_sum = carry
            at = rows_of(number, 32)
            value = resid[at, :]
            normed, scaling = norm_stats(value)
            act[at, :] = (value + (acc[at, :] + bias_down)).astype(bf16)
            incoming = gres[at, :]
            back = norm_back(incoming, normed, scaling, gain_two)
            cotangent = cw[at, :].astype(f32)
            total = cotangent + back
            gres[at, :] = total
            grow[at, :] = total.astype(bf16)
            return (
                gain_sum + col_sum(incoming * normed),
                shift_sum + col_sum(incoming),
                resid_sum + col_sum(total),
                cot_sum + col_sum(cotangent),
            )

        zero_row = jnp.zeros((1, D), f32)
        sums[1:2, :], sums[6:7, :], sums[5:6, :], sums[7:8, :] = lax.fori_loop(
            0, ROWS // 32, second_back, (zero_row,) * 4
        )
        result = t_dot(perm[...], act[...]).astype(bf16)
        for row in range(SIDE):
            out[0, row] = result[row * STRIP : row * STRIP + SIDE, :]

        wgrad[3] = t_dot(mixed[...], grow[...]).astype(bf16)
        mgrad[...] = dot_t(grow[...], weights[3]).astype(bf16)
        sums[3:4, :] = zero_row
        sums[4:5, :] = zero_row
        rel_sum[...] = jnp.zeros_like(rel_sum)

        def attend_back(window, carry):
            at = rows_of(window, PAD)
            for group in range(GROUPS):
                lanes = slice(group * LANES, (group + 1) * LANES)
                wide = slice(group * WIDE, (group + 1) * WIDE)
                mixed_blk = spread_heads(mgrad[at, lanes])
                query_blk = spread_heads(qkv[0, at, lanes])
                prob = dot_t(qkv[2, at, lanes], mixed_blk)
                attention = att[window, group]
                score = attention * (prob - col_sum(attention * prob))
                rel_sum[:, wide] += score
                low = score.astype(bf16)
                value_grad = dot(att_low[window, group], mixed_blk)
                key_grad = score_scale * dot(low, query_blk)
                query_grad = score_scale * join_heads(t_dot(low, qkv[1, at, lanes]))
                sums[3:4, lanes] += col_sum(query_grad)
                sums[4:5, lanes] += col_sum(value_grad)
                dqkv[0, at, lanes] = query_grad.astype(bf16)
                dqkv[1, at, lanes] = key_grad.astype(bf16)
                dqkv[2, at, lanes] = value_grad.astype(bf16)
            return carry

        lax.fori_loop(0, WINDOWS, attend_back, 0)

        for part in range(3):
            wgrad[part] = t_dot(in_one[...], dqkv[part]).astype(bf16)

        base = 0
        for number, count in enumerate(out_counts):

            def store(slot, carry, number=number, base=base):
                target = grads[number].at[slot]

                def make(block, row):
                    row = pl.multiple_of(row, PIECE)
                    pltpu.make_async_copy(
                        wgrad.at[block, pl.ds(row, PIECE)], target, sem_out
                    ).start()

                def make_up(row):
                    row = pl.multiple_of(row, UP_ROWS)
                    for j in range(FF // D):
                        pltpu.make_async_copy(
                            wgrad.at[4 + j, pl.ds(row, UP_ROWS)],
                            target.at[pl.ds(j * UP_ROWS, UP_ROWS)],
                            sem_out,
                        ).start()

                place(out_slots[base + slot], make, make_up)
                return carry

            lax.fori_loop(0, count, store, 0)
            base += count

        acc[...] = dot_t(dqkv[0], weights[0])
        acc[...] += dot_t(dqkv[1], weights[1])
        acc[...] += dot_t(dqkv[2], weights[2])

        def first_back(number, carry):
            gain_sum, shift_sum = carry
            at = rows_of(number, 32)
            normed, scaling = norm_stats(xw[at, :])
            incoming = acc[at, :]
            back = norm_back(incoming, normed, scaling, gain_one)
            act[at, :] = (gres[at, :] + back).astype(bf16)
            return gain_sum + col_sum(incoming * normed), shift_sum + col_sum(incoming)

        sums[0:1, :], sums[2:3, :] = lax.fori_loop(0, ROWS // 32, first_back, (zero_row,) * 2)
        result = t_dot(perm[...], act[...]).astype(bf16)
        for row in range(SIDE):
            in_grad[0, row] = result[row * STRIP : row * STRIP + SIDE, :]
        pltpu.make_async_copy(wgrad, wgrad, sem_out).wait()

    return body


def run_layer(images, cotangent, small, bias, mask, slots, out_slots, pieces, outs):
    perm = jnp.asarray(permutation(), bf16)
    vmem = pl.BlockSpec(memory_space=pltpu.VMEM)
    smem = pl.BlockSpec(memory_space=pltpu.SMEM)
    hbm = pl.BlockSpec(memory_space=pl.ANY)
    counts = [piece.shape[0] for piece in pieces]
    image_shape = (1, SIDE, SIDE, D)
    return pl.pallas_call(
        layer_kernel(counts, outs),
        in_specs=[smem, smem] + [vmem] * 6 + [hbm] * len(counts),
        out_specs=[vmem] * 4 + [hbm] * len(outs),
        out_shape=[
            jax.ShapeDtypeStruct(image_shape, bf16),
            jax.ShapeDtypeStruct(image_shape, bf16),
            jax.ShapeDtypeStruct((SMALL_ROWS, D), f32),
            jax.ShapeDtypeStruct((PAD, HEADS * PAD), f32),
        ]
        + [jax.ShapeDtypeStruct((count, PIECE, D), bf16) for count in outs],
        scratch_shapes=[
            pltpu.VMEM((KINDS, D, D), bf16),
            pltpu.VMEM((KINDS, D, D), bf16),
            pltpu.VMEM((FLAT, D), bf16),
            pltpu.VMEM((ROWS, D), f32),
            pltpu.VMEM((ROWS, D), bf16),
            pltpu.VMEM((ROWS, D), bf16),
            pltpu.VMEM((3, ROWS, D), bf16),
            pltpu.VMEM((WINDOWS, GROUPS, PAD, WIDE), f32),
            pltpu.VMEM((WINDOWS, GROUPS, PAD, WIDE), bf16),
            pltpu.VMEM((ROWS, D), bf16),
            pltpu.VMEM((ROWS, D), f32),
            pltpu.VMEM((ROWS, D), bf16),
            pltpu.VMEM((ROWS, D), bf16),
            pltpu.VMEM((ROWS, D), f32),
            pltpu.VMEM((ROWS, D), f32),
            pltpu.VMEM((ROWS, D), f32),
            pltpu.VMEM((ROWS, D), f32),
            pltpu.VMEM((ROWS, D), bf16),
            pltpu.VMEM((ROWS, D), bf16),
            pltpu.VMEM((3, ROWS, D), bf16),
            pltpu.VMEM((WINDOWS, GROUPS, PAD, WIDE), f32),
            pltpu.SemaphoreType.DMA,
            pltpu.SemaphoreType.DMA,
        ],
        name="layer",
    )(slots, out_slots, images, cotangent, perm, small, bias, mask, *pieces)


VIEW = PIECE * D * 3 // 128


def shard_kinds(device):
    third = 3 * device + jnp.arange(3, dtype=jnp.int32)
    is_up = (third >= PROJ_END) & (third < UP_END)
    return jnp.where(third < QKV_END, 0, jnp.where(is_up, 2, 1)).astype(jnp.int32)


def piece_rows(kind, part):
    per_row = D // 128
    if kind == 0:
        return [(slice(0, PIECE), per_row * part, 3 * per_row)]
    if kind == 1:
        return [(slice(0, PIECE), per_row * PIECE * part, per_row)]
    return [
        (slice(j * UP_ROWS, (j + 1) * UP_ROWS), per_row * (PIECE * part + j), per_row * (FF // D))
        for j in range(FF // D)
    ]


def pack_kernel(kinds, shard, out):
    for part in range(3):
        for kind in range(3):

            @pl.when(kinds[part] == kind)
            def _(part=part, kind=kind):
                for rows, start, stride in piece_rows(kind, part):
                    size = rows.stop - rows.start
                    for lane in range(D // 128):
                        lanes = slice(lane * 128, (lane + 1) * 128)
                        value = shard[pl.ds(start + lane, size, stride=stride), :].astype(bf16)
                        out[part, rows, lanes] = value


def pack_shard(shard, kinds):
    vmem = pl.BlockSpec(memory_space=pltpu.VMEM)
    return pl.pallas_call(
        pack_kernel,
        in_specs=[pl.BlockSpec(memory_space=pltpu.SMEM), vmem],
        out_specs=vmem,
        out_shape=jax.ShapeDtypeStruct((3, PIECE, D), bf16),
        name="pack",
    )(kinds, shard.reshape(VIEW, 128))


def adam_step(weights, first_moment, second_moment, gradient, rate, decay):
    new_first = beta_one * first_moment + (1.0 - beta_one) * gradient
    new_second = beta_two * second_moment + (1.0 - beta_two) * gradient * gradient
    first_hat = new_first / (1.0 - beta_one**STEP)
    second_hat = new_second / (1.0 - beta_two**STEP)
    update = first_hat / (jnp.sqrt(second_hat) + adam_eps) + decay * weights
    return (weights - rate * update, new_first, new_second)


def adam_kernel(grad_scale):
    def body(kinds, *refs):
        mine, theirs, weights, first, second = refs[:5]
        grad, new_weights, new_first, new_second = refs[5:9]
        for part in range(3):
            for kind in range(3):

                @pl.when(kinds[part] == kind)
                def _(part=part, kind=kind):
                    for rows, start, stride in piece_rows(kind, part):
                        size = rows.stop - rows.start
                        for lane in range(D // 128):
                            lanes = slice(lane * 128, (lane + 1) * 128)
                            total = mine[part, rows, lanes].astype(f32) + theirs[
                                part, rows, lanes
                            ].astype(f32)
                            grad[pl.ds(start + lane, size, stride=stride), :] = total * grad_scale

        def step(number, carry):
            at = pl.ds(pl.multiple_of(number * 64, 64), 64)
            new_weights[at, :], new_first[at, :], new_second[at, :] = adam_step(
                weights[at, :], first[at, :], second[at, :], grad[at, :], rate_matrix, decay_rate
            )
            return carry

        lax.fori_loop(0, VIEW // 64, step, 0)

    return body


def adam_shard(kinds, parts, weights, first, second, grad_scale):
    vmem = pl.BlockSpec(memory_space=pltpu.VMEM)
    size = weights.shape[0]
    results = pl.pallas_call(
        adam_kernel(grad_scale),
        in_specs=[pl.BlockSpec(memory_space=pltpu.SMEM)] + [vmem] * 5,
        out_specs=[vmem] * 4,
        out_shape=[jax.ShapeDtypeStruct((VIEW, 128), f32)] * 4,
        name="adam",
    )(kinds, *parts, *(array.reshape(VIEW, 128) for array in (weights, first, second)))
    return [result.reshape(size) for result in results]


def to_pieces(flat):
    q_end, p_end, u_end = QKV_END * PIECE * D, PROJ_END * PIECE * D, UP_END * PIECE * D
    qkv = flat[:q_end].reshape(-1, PIECE, 3, D).transpose(0, 2, 1, 3).reshape(-1, PIECE, D)
    proj = flat[q_end:p_end].reshape(-1, PIECE, D)
    up = flat[p_end:u_end].reshape(-1, UP_ROWS, FF // D, D).transpose(0, 2, 1, 3)
    down = flat[u_end:].reshape(-1, PIECE, D)
    return jnp.concatenate([qkv, proj, up.reshape(-1, PIECE, D), down])


def from_pieces(pieces):
    qkv = pieces[:QKV_END].reshape(-1, 3, PIECE, D).transpose(0, 2, 1, 3)
    up = pieces[PROJ_END:UP_END].reshape(-1, FF // D, UP_ROWS, D).transpose(0, 2, 1, 3)
    return jnp.concatenate(
        [
            qkv.reshape(-1),
            pieces[QKV_END:PROJ_END].reshape(-1),
            up.reshape(-1),
            pieces[UP_END:].reshape(-1),
        ]
    )


def offset_grid():
    spots = np.arange(PAD)
    rows_at = spots // WIN
    cols_at = spots % WIN
    grid = (rows_at[None, :] - rows_at[:, None] + WIN - 1) * (2 * WIN - 1) + (
        cols_at[None, :] - cols_at[:, None] + WIN - 1
    )
    real = (spots[:, None] < PLACES) & (spots[None, :] < PLACES)
    return np.where(real, grid, -1)


AXES = ("rep", "grp")


def on_device(
    images, cotangent, region_ids, rel_index, matrices, matrix_m, matrix_v, small, small_m, small_v
):
    devices = lax.axis_size("rep") * lax.axis_size("grp")
    me = lax.axis_index(AXES)
    bits = [1 << number for number in range(devices.bit_length() - 1)]
    exact = devices == sum(bits) + 1 and matrices.shape[0] == 3 * PIECE * D

    def swap(value, bit):
        return lax.ppermute(value, AXES, [(i, i ^ bit) for i in range(devices)])

    labels = jnp.arange(REL, dtype=jnp.int32)
    grid = jnp.asarray(offset_grid(), jnp.int32)

    def split(values):
        high = lax.reduce_precision(values, 8, 7)
        middle = lax.reduce_precision(values - high, 8, 7)
        low = values - high - middle
        return [part.astype(bf16) for part in (high, middle, low)]

    def tables(rel_index):
        select_offset = (grid[None] == labels[:, None, None]).astype(f32)
        select_row = (rel_index[:, None] == labels[None, :]).astype(f32)
        return select_offset, select_row

    def prepare(small, region_ids, rel_index):
        small_rows = small[: SMALL_ROWS * D].reshape(SMALL_ROWS, D)
        rel_table = small[SMALL_ROWS * D :].reshape(REL, HEADS)
        select_offset, select_row = tables(rel_index)
        table_rows = jnp.dot(select_row, rel_table, precision=highest)
        table_parts = jnp.concatenate(split(table_rows), axis=1)
        bias = jnp.einsum(
            "okq,oh->khq", select_offset.astype(bf16), table_parts, preferred_element_type=f32
        )
        bias = bias.reshape(PAD, 3, HEADS, PAD).sum(axis=1)
        blocks = SIDE // WIN
        regions = region_ids.reshape(blocks, WIN, blocks, WIN).transpose(0, 2, 1, 3)
        regions = regions.reshape(WINDOWS, PLACES)
        padded = ((0, 0), (0, PAD - PLACES))
        keys = jnp.pad(regions, padded, constant_values=-1)[:, :, None]
        queries = jnp.tile(jnp.pad(regions, padded, constant_values=-2), (1, GROUP))[:, None, :]
        mask = (keys == queries).astype(jnp.int32)
        return small_rows, bias.reshape(PAD, HEADS * PAD), mask

    if exact:
        core, inner, top = bits[0], bits[1:-1], bits[-1]
        orders = [inner[color:] + inner[:color] for color in range(3)]
        kinds = shard_kinds(me)
        packed = pack_shard(matrices, kinds)
        received = swap(packed, top)
        masks = [[0]] * 3 + [[top]] * 3
        for color in range(3):
            for step in range(1, len(inner)):
                for at in (color, 3 + color):
                    bit = orders[color][-step]
                    masks[at] = masks[at] + [mask ^ bit for mask in masks[at]]

        def slot_table(entries):
            table = jnp.asarray(entries, jnp.int32)
            return 3 * (me ^ table[:, 0]) + table[:, 1]

        out_entries = []
        for color in range(3):
            order = orders[color] + [top]
            half = [0]
            for bit in reversed(order[1:]):
                half = half + [mask ^ bit for mask in half]
            for extra in (order[0] ^ core, core, order[0], 0):
                out_entries += [(mask ^ extra, color) for mask in half]
        piece_entries = []
        for tree in range(2):
            for color in range(3):
                last = orders[color][0]
                for extra in (0, last, core, last ^ core):
                    piece_entries += [(mask ^ extra, color) for mask in masks[3 * tree + color]]
        operands = prepare(small, region_ids, rel_index)
        operands = (*operands, slot_table(piece_entries), slot_table(out_entries))
        received, operands = lax.optimization_barrier((received, operands))
        buffers = [tree[color : color + 1] for tree in (packed, received) for color in range(3)]
        for step, tree in ((1, 0), (1, 1), (2, 0), (2, 1)):
            for color in range(3):
                at = 3 * tree + color
                bit = orders[color][-step]
                own = buffers[at]
                other = swap(own, bit)
                buffers[at] = jnp.concatenate([own, other])

        pieces = []
        for tree in range(2):
            for color in range(3):
                buffer = buffers[3 * tree + color]
                far = swap(buffer, orders[color][0])
                pieces += [buffer, far, swap(buffer, core), swap(far, core)]
        outs = [devices // 4] * 12
    else:
        gathered = lax.all_gather(matrices.astype(bf16), AXES, axis=0, tiled=True)
        pieces = [to_pieces(gathered)]
        slots = jnp.arange(BLOCKS, dtype=jnp.int32)
        operands = (*prepare(small, region_ids, rel_index), slots, slots)
        outs = [BLOCKS]

    output, input_grad, sums, rel_sum, *grads = run_layer(
        images, cotangent, *operands, pieces, outs
    )

    tokens_all = images.shape[0] * devices * SIDE * SIDE
    grad_scale = 1.0 / math.sqrt(tokens_all)

    def small_sums(sums, rel_sum, rel_index):
        select_offset, select_row = tables(rel_index)
        rel_parts = jnp.concatenate(split(rel_sum.reshape(PAD, HEADS, PAD)), axis=1)
        rel_grad = jnp.einsum(
            "okq,khq->oh", select_offset.astype(bf16), rel_parts, preferred_element_type=f32
        )
        rel_grad = rel_grad.reshape(REL, 3, HEADS).sum(axis=1)
        table_grad = jnp.dot(select_row.T, rel_grad, precision=highest)
        return jnp.concatenate([sums.reshape(-1), table_grad.reshape(-1)]) * grad_scale

    if exact:

        def add(a, b):
            return (a.astype(f32) + b.astype(f32)).astype(bf16)

        from_far = [swap(grads[4 * color], core) for color in range(3)]
        from_near = [swap(grads[4 * color + 1], core) for color in range(3)]
        far = [add(grads[4 * color + 2], from_far[color]) for color in range(3)]
        small_grad = small_sums(sums, rel_sum, rel_index)
        near = [add(grads[4 * color + 3], from_near[color]) for color in range(3)]
        for stage in range(3):
            for color in range(3):
                received = swap(far[color], orders[color][stage])
                size = received.shape[0] // 2
                far[color] = add(near[color][size:], received[size:])
                near[color] = add(near[color][:size], received[:size])
        parts = [jnp.concatenate(near), swap(jnp.concatenate(far), top)]
        for bit in bits:
            small_grad = small_grad + swap(small_grad, bit)
        owned_grad, new_matrices, new_matrix_m, new_matrix_v = adam_shard(
            kinds, parts, matrices, matrix_m, matrix_v, grad_scale
        )
    else:
        flat_grad = from_pieces(grads[0].astype(f32)) * grad_scale
        owned_grad = lax.psum_scatter(flat_grad, AXES, scatter_dimension=0, tiled=True)
        new_matrices, new_matrix_m, new_matrix_v = adam_step(
            matrices, matrix_m, matrix_v, owned_grad, rate_matrix, decay_rate
        )
        small_grad = lax.psum(small_sums(sums, rel_sum, rel_index), AXES)
    new_small, new_small_m, new_small_v = adam_step(
        small, small_m, small_v, small_grad, rate_small, 0.0
    )
    return (
        output,
        input_grad,
        owned_grad,
        small_grad,
        new_matrices,
        new_matrix_m,
        new_matrix_v,
        new_small,
        new_small_m,
        new_small_v,
    )


def solution(mesh):
    tokens = P(AXES, None, None, None)
    shard = P(AXES)
    whole = P()

    return jax.shard_map(
        on_device,
        mesh=mesh,
        in_specs=(tokens, tokens, whole, whole, shard, shard, shard, whole, whole, whole),
        out_specs=(tokens, tokens, shard, whole, shard, shard, shard, whole, whole, whole),
        check_vma=False,
    )
```

```python
import math

import jax
import jax.numpy as jnp
import numpy as np
from jax import lax
from jax.experimental import pallas as pl
from jax.experimental.pallas import tpu as pltpu
from jax.sharding import PartitionSpec as P


D = 512
HEADS = 16
FF = 2048
WIN = 7
SIDE = 14
SHIFT = 3
STEP = 5
HEAD_DIM = 32
REL = 169

norm_eps = 1e-05
beta_one = 0.9
beta_two = 0.999
adam_eps = 1e-08
rate_matrix = 0.01
rate_small = 0.2
decay_rate = 0.05
masked_score = -1e30
root_half = 0.7071067811865476
inv_root_twopi = 0.3989422804014327
highest = lax.Precision.HIGHEST
score_scale = HEAD_DIM ** (-0.5)

PLACES = WIN * WIN
PAD = 64
WINDOWS = (SIDE // WIN) ** 2
ROWS = WINDOWS * PAD
STRIP = 16
FLAT = SIDE * STRIP
GROUP = 4
GROUPS = HEADS // GROUP
LANES = GROUP * HEAD_DIM
WIDE = GROUP * PAD

PIECE = 64
UP_ROWS = PIECE // (FF // D)
BLOCKS = (3 * D * D + D * D + 2 * D * FF) // (PIECE * D)
QKV_END = 3 * D // PIECE
PROJ_END = QKV_END + D // PIECE
UP_END = PROJ_END + FF // PIECE
SMALL_ROWS = 8 + FF // D
f32 = jnp.float32
bf16 = jnp.bfloat16


def window_source():
    source = np.full((ROWS,), -1, np.int64)
    blocks = SIDE // WIN
    for window in range(WINDOWS):
        for place in range(PLACES):
            row = (window // blocks * WIN + place // WIN + SHIFT) % SIDE
            col = (window % blocks * WIN + place % WIN + SHIFT) % SIDE
            source[window * PAD + place] = row * STRIP + col
    return source


def permutation():
    return (window_source()[:, None] == np.arange(FLAT)[None, :]).astype(np.float32)


def dot(a, b):
    return lax.dot_general(a, b, (((1,), (0,)), ((), ())), preferred_element_type=f32)


def dot_t(a, b):
    return lax.dot_general(a, b, (((1,), (1,)), ((), ())), preferred_element_type=f32)


def t_dot(a, b):
    return lax.dot_general(a, b, (((0,), (0,)), ((), ())), preferred_element_type=f32)


def norm_stats(values):
    center = values - jnp.mean(values, axis=-1, keepdims=True)
    spread = jnp.mean(center * center, axis=-1, keepdims=True)
    scaling = lax.rsqrt(spread + norm_eps)
    return center * scaling, scaling


def norm_back(incoming, normed, scaling, gain_vector):
    scaled = incoming * gain_vector
    return scaling * (
        scaled
        - jnp.mean(scaled, axis=-1, keepdims=True)
        - normed * jnp.mean(scaled * normed, axis=-1, keepdims=True)
    )


def col_sum(values):
    return jnp.sum(values, axis=0, keepdims=True)


def layer_kernel(counts, out_counts):
    n_in = len(counts)
    n_out = len(out_counts)

    def body(*refs):
        slots, out_slots = refs[0], refs[1]
        img, cot, perm, small, bias, mask = refs[2:8]
        pieces = refs[8 : 8 + n_in]
        refs = refs[8 + n_in :]
        out, in_grad, sums, rel_sum = refs[:4]
        grads = refs[4 : 4 + n_out]
        (
            weights,
            wgrad,
            n_one,
            n_two,
            s_one,
            s_two,
            flat,
            xw,
            cw,
            in_one,
            qkv,
            att,
            att_low,
            mixed,
            resid,
            in_two,
            act,
            acc,
            acc_two,
            pre,
            gres,
            grow,
            mgrad,
            dqkv,
            ext,
            sem,
            sem_out,
        ) = refs[4 + n_out :]

        base = 0
        for number, count in enumerate(counts):

            def fetch(slot, carry, number=number, base=base):
                pltpu.make_async_copy(
                    pieces[number].at[slot], weights.at[slots[base + slot]], sem
                ).start()
                return carry

            lax.fori_loop(0, count, fetch, 0, unroll=min(count, 8))
            base += count

        def third_rows(first, count, stride=1):
            parts = [weights[first + stride * number] for number in range(count)]
            return jnp.concatenate(parts, axis=0)

        def qkv_block(part):
            return third_rows(part, D // PIECE, 3)

        def proj_block():
            return weights[QKV_END:PROJ_END].reshape(D, D)

        def up_block(j):
            at = pl.ds(pl.multiple_of(j * UP_ROWS, UP_ROWS), UP_ROWS)
            return weights[PROJ_END:UP_END, at, :].reshape(D, D)

        def down_block(j):
            return weights[pl.ds(UP_END + j * (D // PIECE), D // PIECE)].reshape(D, D)

        gain_one, gain_two, shift_one, bias_query, bias_value, bias_proj, shift_two, bias_down = (
            small[number : number + 1, :] for number in range(8)
        )

        flat[...] = jnp.zeros_like(flat)
        for row in range(SIDE):
            flat[row * STRIP : row * STRIP + SIDE, :] = img[0, row]
        xw[...] = dot(perm[...], flat[...])
        for row in range(SIDE):
            flat[row * STRIP : row * STRIP + SIDE, :] = cot[0, row]
        cw[...] = dot(perm[...], flat[...]).astype(bf16)

        def rows_of(number, size):
            return pl.ds(pl.multiple_of(number * size, size), size)

        def norm_one(number, carry):
            at = rows_of(number, PAD)
            normed, scaling = norm_stats(xw[at, :])
            n_one[at, :] = normed
            s_one[at, :] = jnp.broadcast_to(scaling, (PAD, 128))
            in_one[at, :] = (normed * gain_one + shift_one).astype(bf16)
            return carry

        lax.fori_loop(0, WINDOWS, norm_one, 0, unroll=True)

        for window in range(WINDOWS):
            allowed = mask[window] != 0
            for group in range(GROUPS):
                ext[window, group] = jnp.where(
                    allowed, bias[:, group * WIDE : (group + 1) * WIDE], masked_score
                )
        head_mask = (
            lax.broadcasted_iota(jnp.int32, (WIDE, LANES), 0) // PAD
            == lax.broadcasted_iota(jnp.int32, (WIDE, LANES), 1) // HEAD_DIM
        )

        def spread_heads(values):
            return jnp.where(head_mask, jnp.concatenate([values] * GROUP, axis=0), 0)

        def join_heads(values):
            kept = jnp.where(head_mask, values, 0.0)
            total = kept[:PAD]
            for head in range(1, GROUP):
                total = total + kept[head * PAD : (head + 1) * PAD]
            return total

        pltpu.make_async_copy(weights, weights, sem).wait()

        for part, vector in enumerate((bias_query, None, bias_value)):
            product = dot(in_one[...], qkv_block(part))
            if vector is not None:
                product = product + vector
            qkv[part] = product.astype(bf16)

        def attend(window, carry):
            at = rows_of(window, PAD)
            for group in range(GROUPS):
                lanes = slice(group * LANES, (group + 1) * LANES)
                scores = dot_t(qkv[1, at, lanes], spread_heads(qkv[0, at, lanes]))
                masked = score_scale * scores + ext[window, group]
                top = jnp.max(masked, axis=0, keepdims=True)
                raised = jnp.exp(masked - top)
                attention = raised * (1.0 / col_sum(raised))
                low = attention.astype(bf16)
                att[window, group] = attention
                att_low[window, group] = low
                mixed[at, lanes] = join_heads(t_dot(low, qkv[2, at, lanes])).astype(bf16)
            return carry

        lax.fori_loop(0, WINDOWS, attend, 0)

        resid[...] = xw[...] + (dot(mixed[...], proj_block()) + bias_proj)

        def norm_two(number, carry):
            at = rows_of(number, PAD)
            normed, scaling = norm_stats(resid[at, :])
            n_two[at, :] = normed
            s_two[at, :] = jnp.broadcast_to(scaling, (PAD, 128))
            in_two[at, :] = (normed * gain_two + shift_two).astype(bf16)
            return carry

        lax.fori_loop(0, WINDOWS, norm_two, 0, unroll=True)

        def feed(j, carry):
            acc_two[...] = dot(in_two[...], up_block(j)) + small[pl.ds(8 + j, 1), :]
            pre[...] = dot_t(cw[...], down_block(j))

            def gelu_part(number, total):
                at = rows_of(number, 32)
                value = acc_two[at, :]
                phi = 0.5 * (1.0 + lax.erf(value * root_half))
                act[at, :] = (value * phi).astype(bf16)
                slope = phi + value * jnp.exp(-0.5 * value * value) * inv_root_twopi
                back = pre[at, :] * slope
                grow[at, :] = back.astype(bf16)
                return total + col_sum(back)

            sums[pl.ds(8 + j, 1), :] = lax.fori_loop(
                0, ROWS // 32, gelu_part, jnp.zeros((1, D), f32), unroll=2
            )
            forward = dot(act[...], down_block(j))
            backward = dot_t(grow[...], up_block(j))

            @pl.when(j == 0)
            def _():
                acc[...] = forward
                gres[...] = backward

            @pl.when(j > 0)
            def _():
                acc[...] += forward
                gres[...] += backward

            up_grad = t_dot(in_two[...], grow[...]).astype(bf16)
            at = pl.ds(pl.multiple_of(j * UP_ROWS, UP_ROWS), UP_ROWS)
            wgrad[PROJ_END:UP_END, at, :] = up_grad.reshape(FF // PIECE, UP_ROWS, D)
            down_grad = t_dot(act[...], cw[...]).astype(bf16)
            wgrad[pl.ds(UP_END + j * (D // PIECE), D // PIECE)] = down_grad.reshape(
                D // PIECE, PIECE, D
            )
            return carry

        lax.fori_loop(0, FF // D, feed, 0)

        def second_back(number, carry):
            gain_sum, shift_sum, resid_sum, cot_sum = carry
            at = rows_of(number, 32)
            value = resid[at, :]
            normed, scaling = n_two[at, :], s_two[at, 0:1]
            act[at, :] = (value + (acc[at, :] + bias_down)).astype(bf16)
            incoming = gres[at, :]
            back = norm_back(incoming, normed, scaling, gain_two)
            cotangent = cw[at, :].astype(f32)
            total = cotangent + back
            gres[at, :] = total
            grow[at, :] = total.astype(bf16)
            return (
                gain_sum + col_sum(incoming * normed),
                shift_sum + col_sum(incoming),
                resid_sum + col_sum(total),
                cot_sum + col_sum(cotangent),
            )

        zero_row = jnp.zeros((1, D), f32)
        sums[1:2, :], sums[6:7, :], sums[5:6, :], sums[7:8, :] = lax.fori_loop(
            0, ROWS // 32, second_back, (zero_row,) * 4, unroll=4
        )
        result = t_dot(perm[...], act[...]).astype(bf16)
        for row in range(SIDE):
            out[0, row] = result[row * STRIP : row * STRIP + SIDE, :]

        proj_grad = t_dot(mixed[...], grow[...]).astype(bf16)
        wgrad[QKV_END:PROJ_END] = proj_grad.reshape(D // PIECE, PIECE, D)
        mgrad[...] = dot_t(grow[...], proj_block()).astype(bf16)
        sums[3:4, :] = zero_row
        sums[4:5, :] = zero_row
        rel_sum[...] = jnp.zeros_like(rel_sum)

        def attend_back(window, carry):
            at = rows_of(window, PAD)
            for group in range(GROUPS):
                lanes = slice(group * LANES, (group + 1) * LANES)
                wide = slice(group * WIDE, (group + 1) * WIDE)
                mixed_blk = spread_heads(mgrad[at, lanes])
                query_blk = spread_heads(qkv[0, at, lanes])
                prob = dot_t(qkv[2, at, lanes], mixed_blk)
                attention = att[window, group]
                score = attention * (prob - col_sum(attention * prob))
                rel_sum[:, wide] += score
                low = score.astype(bf16)
                value_grad = dot(att_low[window, group], mixed_blk)
                key_grad = score_scale * dot(low, query_blk)
                query_grad = score_scale * join_heads(t_dot(low, qkv[1, at, lanes]))
                sums[3:4, lanes] += col_sum(query_grad)
                sums[4:5, lanes] += col_sum(value_grad)
                dqkv[0, at, lanes] = query_grad.astype(bf16)
                dqkv[1, at, lanes] = key_grad.astype(bf16)
                dqkv[2, at, lanes] = value_grad.astype(bf16)
            return carry

        lax.fori_loop(0, WINDOWS, attend_back, 0)

        for part in range(3):
            part_grad = t_dot(in_one[...], dqkv[part]).astype(bf16)
            for number in range(D // PIECE):
                wgrad[3 * number + part] = part_grad[number * PIECE : (number + 1) * PIECE]

        base = 0
        for number, count in enumerate(out_counts):

            def store(slot, carry, number=number, base=base):
                pltpu.make_async_copy(
                    wgrad.at[out_slots[base + slot]], grads[number].at[slot], sem_out
                ).start()
                return carry

            lax.fori_loop(0, count, store, 0, unroll=min(count, 8))
            base += count

        acc[...] = (
            dot_t(dqkv[0], qkv_block(0)) + dot_t(dqkv[1], qkv_block(1))
        ) + dot_t(dqkv[2], qkv_block(2))

        def first_back(number, carry):
            gain_sum, shift_sum = carry
            at = rows_of(number, 32)
            normed, scaling = n_one[at, :], s_one[at, 0:1]
            incoming = acc[at, :]
            back = norm_back(incoming, normed, scaling, gain_one)
            act[at, :] = (gres[at, :] + back).astype(bf16)
            return gain_sum + col_sum(incoming * normed), shift_sum + col_sum(incoming)

        sums[0:1, :], sums[2:3, :] = lax.fori_loop(
            0, ROWS // 32, first_back, (zero_row,) * 2, unroll=4
        )
        result = t_dot(perm[...], act[...]).astype(bf16)
        for row in range(SIDE):
            in_grad[0, row] = result[row * STRIP : row * STRIP + SIDE, :]
        pltpu.make_async_copy(wgrad, wgrad, sem_out).wait()

    return body


def run_layer(images, cotangent, small, bias, mask, slots, out_slots, pieces, outs):
    perm = jnp.asarray(permutation(), bf16)
    vmem = pl.BlockSpec(memory_space=pltpu.VMEM)
    smem = pl.BlockSpec(memory_space=pltpu.SMEM)
    hbm = pl.BlockSpec(memory_space=pl.ANY)
    counts = [piece.shape[0] for piece in pieces]
    image_shape = (1, SIDE, SIDE, D)
    return pl.pallas_call(
        layer_kernel(counts, outs),
        in_specs=[smem, smem] + [vmem] * 6 + [hbm] * len(counts),
        out_specs=[vmem] * 4 + [hbm] * len(outs),
        out_shape=[
            jax.ShapeDtypeStruct(image_shape, bf16),
            jax.ShapeDtypeStruct(image_shape, bf16),
            jax.ShapeDtypeStruct((SMALL_ROWS, D), f32),
            jax.ShapeDtypeStruct((PAD, HEADS * PAD), f32),
        ]
        + [jax.ShapeDtypeStruct((count, PIECE, D), bf16) for count in outs],
        scratch_shapes=[
            pltpu.VMEM((BLOCKS, PIECE, D), bf16),
            pltpu.VMEM((BLOCKS, PIECE, D), bf16),
            pltpu.VMEM((ROWS, D), f32),
            pltpu.VMEM((ROWS, D), f32),
            pltpu.VMEM((ROWS, 128), f32),
            pltpu.VMEM((ROWS, 128), f32),
            pltpu.VMEM((FLAT, D), bf16),
            pltpu.VMEM((ROWS, D), f32),
            pltpu.VMEM((ROWS, D), bf16),
            pltpu.VMEM((ROWS, D), bf16),
            pltpu.VMEM((3, ROWS, D), bf16),
            pltpu.VMEM((WINDOWS, GROUPS, PAD, WIDE), f32),
            pltpu.VMEM((WINDOWS, GROUPS, PAD, WIDE), bf16),
            pltpu.VMEM((ROWS, D), bf16),
            pltpu.VMEM((ROWS, D), f32),
            pltpu.VMEM((ROWS, D), bf16),
            pltpu.VMEM((ROWS, D), bf16),
            pltpu.VMEM((ROWS, D), f32),
            pltpu.VMEM((ROWS, D), f32),
            pltpu.VMEM((ROWS, D), f32),
            pltpu.VMEM((ROWS, D), f32),
            pltpu.VMEM((ROWS, D), bf16),
            pltpu.VMEM((ROWS, D), bf16),
            pltpu.VMEM((3, ROWS, D), bf16),
            pltpu.VMEM((WINDOWS, GROUPS, PAD, WIDE), f32),
            pltpu.SemaphoreType.DMA,
            pltpu.SemaphoreType.DMA,
        ],
        name="layer",
    )(slots, out_slots, images, cotangent, perm, small, bias, mask, *pieces)


VIEW = PIECE * D * 3 // 128


def shard_kinds(device):
    third = 3 * device + jnp.arange(3, dtype=jnp.int32)
    is_up = (third >= PROJ_END) & (third < UP_END)
    return jnp.where(third < QKV_END, 0, jnp.where(is_up, 2, 1)).astype(jnp.int32)


def piece_rows(kind, part):
    per_row = D // 128
    if kind == 0:
        return [(slice(0, PIECE), per_row * part, 3 * per_row)]
    if kind == 1:
        return [(slice(0, PIECE), per_row * PIECE * part, per_row)]
    return [
        (slice(j * UP_ROWS, (j + 1) * UP_ROWS), per_row * (PIECE * part + j), per_row * (FF // D))
        for j in range(FF // D)
    ]


def pack_kernel(kinds, shard, out):
    for part in range(3):
        for kind in range(3):

            @pl.when(kinds[part] == kind)
            def _(part=part, kind=kind):
                for rows, start, stride in piece_rows(kind, part):
                    size = rows.stop - rows.start
                    for lane in range(D // 128):
                        lanes = slice(lane * 128, (lane + 1) * 128)
                        value = shard[pl.ds(start + lane, size, stride=stride), :].astype(bf16)
                        out[part, rows, lanes] = value


def pack_shard(shard, kinds):
    vmem = pl.BlockSpec(memory_space=pltpu.VMEM)
    return pl.pallas_call(
        pack_kernel,
        in_specs=[pl.BlockSpec(memory_space=pltpu.SMEM), vmem],
        out_specs=vmem,
        out_shape=jax.ShapeDtypeStruct((3, PIECE, D), bf16),
        name="pack",
    )(kinds, shard.reshape(VIEW, 128))


def adam_step(weights, first_moment, second_moment, gradient, rate, decay):
    new_first = beta_one * first_moment + (1.0 - beta_one) * gradient
    new_second = beta_two * second_moment + (1.0 - beta_two) * gradient * gradient
    first_hat = new_first / (1.0 - beta_one**STEP)
    second_hat = new_second / (1.0 - beta_two**STEP)
    update = first_hat / (jnp.sqrt(second_hat) + adam_eps) + decay * weights
    return (weights - rate * update, new_first, new_second)


def adam_kernel(grad_scale):
    def body(kinds, *refs):
        mine, theirs, weights, first, second = refs[:5]
        grad, new_weights, new_first, new_second = refs[5:9]
        for part in range(3):
            for kind in range(3):

                @pl.when(kinds[part] == kind)
                def _(part=part, kind=kind):
                    for rows, start, stride in piece_rows(kind, part):
                        size = rows.stop - rows.start
                        for lane in range(D // 128):
                            lanes = slice(lane * 128, (lane + 1) * 128)
                            total = mine[part, rows, lanes].astype(f32) + theirs[
                                part, rows, lanes
                            ].astype(f32)
                            grad[pl.ds(start + lane, size, stride=stride), :] = total * grad_scale

        def step(number, carry):
            at = pl.ds(pl.multiple_of(number * 64, 64), 64)
            new_weights[at, :], new_first[at, :], new_second[at, :] = adam_step(
                weights[at, :], first[at, :], second[at, :], grad[at, :], rate_matrix, decay_rate
            )
            return carry

        lax.fori_loop(0, VIEW // 64, step, 0)

    return body


def adam_shard(kinds, parts, weights, first, second, grad_scale):
    vmem = pl.BlockSpec(memory_space=pltpu.VMEM)
    size = weights.shape[0]
    results = pl.pallas_call(
        adam_kernel(grad_scale),
        in_specs=[pl.BlockSpec(memory_space=pltpu.SMEM)] + [vmem] * 5,
        out_specs=[vmem] * 4,
        out_shape=[jax.ShapeDtypeStruct((VIEW, 128), f32)] * 4,
        name="adam",
    )(kinds, *parts, *(array.reshape(VIEW, 128) for array in (weights, first, second)))
    return [result.reshape(size) for result in results]


def to_pieces(flat):
    q_end, p_end, u_end = QKV_END * PIECE * D, PROJ_END * PIECE * D, UP_END * PIECE * D
    qkv = flat[:q_end].reshape(-1, PIECE, 3, D).transpose(0, 2, 1, 3).reshape(-1, PIECE, D)
    proj = flat[q_end:p_end].reshape(-1, PIECE, D)
    up = flat[p_end:u_end].reshape(-1, UP_ROWS, FF // D, D).transpose(0, 2, 1, 3)
    down = flat[u_end:].reshape(-1, PIECE, D)
    return jnp.concatenate([qkv, proj, up.reshape(-1, PIECE, D), down])


def from_pieces(pieces):
    qkv = pieces[:QKV_END].reshape(-1, 3, PIECE, D).transpose(0, 2, 1, 3)
    up = pieces[PROJ_END:UP_END].reshape(-1, FF // D, UP_ROWS, D).transpose(0, 2, 1, 3)
    return jnp.concatenate(
        [
            qkv.reshape(-1),
            pieces[QKV_END:PROJ_END].reshape(-1),
            up.reshape(-1),
            pieces[UP_END:].reshape(-1),
        ]
    )


def offset_grid():
    spots = np.arange(PAD)
    rows_at = spots // WIN
    cols_at = spots % WIN
    grid = (rows_at[None, :] - rows_at[:, None] + WIN - 1) * (2 * WIN - 1) + (
        cols_at[None, :] - cols_at[:, None] + WIN - 1
    )
    real = (spots[:, None] < PLACES) & (spots[None, :] < PLACES)
    return np.where(real, grid, -1)


AXES = ("rep", "grp")


def on_device(
    images, cotangent, region_ids, rel_index, matrices, matrix_m, matrix_v, small, small_m, small_v
):
    devices = lax.axis_size("rep") * lax.axis_size("grp")
    me = lax.axis_index(AXES)
    bits = [1 << number for number in range(devices.bit_length() - 1)]
    exact = devices == sum(bits) + 1 and matrices.shape[0] == 3 * PIECE * D

    def swap(value, bit):
        return lax.ppermute(value, AXES, [(i, i ^ bit) for i in range(devices)])

    labels = jnp.arange(REL, dtype=jnp.int32)
    grid = jnp.asarray(offset_grid(), jnp.int32)

    def split(values):
        high = lax.reduce_precision(values, 8, 7)
        middle = lax.reduce_precision(values - high, 8, 7)
        low = values - high - middle
        return [part.astype(bf16) for part in (high, middle, low)]

    def tables(rel_index):
        select_offset = (grid[None] == labels[:, None, None]).astype(f32)
        select_row = (rel_index[:, None] == labels[None, :]).astype(f32)
        return select_offset, select_row

    def prepare(small, region_ids, rel_index):
        small_rows = small[: SMALL_ROWS * D].reshape(SMALL_ROWS, D)
        rel_table = small[SMALL_ROWS * D :].reshape(REL, HEADS)
        select_offset, select_row = tables(rel_index)
        table_rows = jnp.dot(select_row, rel_table, precision=highest)
        table_parts = jnp.concatenate(split(table_rows), axis=1)
        bias = jnp.einsum(
            "okq,oh->khq", select_offset.astype(bf16), table_parts, preferred_element_type=f32
        )
        bias = bias.reshape(PAD, 3, HEADS, PAD).sum(axis=1)
        blocks = SIDE // WIN
        regions = region_ids.reshape(blocks, WIN, blocks, WIN).transpose(0, 2, 1, 3)
        regions = regions.reshape(WINDOWS, PLACES)
        padded = ((0, 0), (0, PAD - PLACES))
        keys = jnp.pad(regions, padded, constant_values=-1)[:, :, None]
        queries = jnp.tile(jnp.pad(regions, padded, constant_values=-2), (1, GROUP))[:, None, :]
        mask = (keys == queries).astype(jnp.int32)
        return small_rows, bias.reshape(PAD, HEADS * PAD), mask

    if exact:
        core, inner, top = bits[0], bits[1:-1], bits[-1]
        orders = [inner[color:] + inner[:color] for color in range(3)]
        kinds = shard_kinds(me)
        packed = pack_shard(matrices, kinds)
        received = swap(packed, top)
        masks = [[0]] * 3 + [[top]] * 3
        for color in range(3):
            for step in range(1, len(inner)):
                for at in (color, 3 + color):
                    bit = orders[color][-step]
                    masks[at] = masks[at] + [mask ^ bit for mask in masks[at]]

        def slot_table(entries):
            table = jnp.asarray(entries, jnp.int32)
            return 3 * (me ^ table[:, 0]) + table[:, 1]

        out_entries = []
        for color in range(3):
            order = orders[color] + [top]
            half = [0]
            for bit in reversed(order[1:]):
                half = half + [mask ^ bit for mask in half]
            for extra in (order[0] ^ core, core, order[0], 0):
                out_entries += [(mask ^ extra, color) for mask in half]
        piece_entries = []
        for tree in range(2):
            for color in range(3):
                last = orders[color][0]
                for extra in (0, last, core, last ^ core):
                    piece_entries += [(mask ^ extra, color) for mask in masks[3 * tree + color]]
        operands = prepare(small, region_ids, rel_index)
        operands = (*operands, slot_table(piece_entries), slot_table(out_entries))
        received, operands = lax.optimization_barrier((received, operands))
        buffers = [tree[color : color + 1] for tree in (packed, received) for color in range(3)]
        for step, tree in ((1, 0), (1, 1), (2, 0), (2, 1)):
            for color in range(3):
                at = 3 * tree + color
                bit = orders[color][-step]
                own = buffers[at]
                other = swap(own, bit)
                buffers[at] = jnp.concatenate([own, other])

        pieces = []
        for tree in range(2):
            for color in range(3):
                buffer = buffers[3 * tree + color]
                far = swap(buffer, orders[color][0])
                pieces += [buffer, far, swap(buffer, core), swap(far, core)]
        outs = [devices // 4] * 12
    else:
        gathered = lax.all_gather(matrices.astype(bf16), AXES, axis=0, tiled=True)
        pieces = [to_pieces(gathered)]
        slots = jnp.arange(BLOCKS, dtype=jnp.int32)
        operands = (*prepare(small, region_ids, rel_index), slots, slots)
        outs = [BLOCKS]

    output, input_grad, sums, rel_sum, *grads = run_layer(
        images, cotangent, *operands, pieces, outs
    )

    tokens_all = images.shape[0] * devices * SIDE * SIDE
    grad_scale = 1.0 / math.sqrt(tokens_all)

    def small_sums(sums, rel_sum, rel_index):
        select_offset, select_row = tables(rel_index)
        rel_parts = jnp.concatenate(split(rel_sum.reshape(PAD, HEADS, PAD)), axis=1)
        rel_grad = jnp.einsum(
            "okq,khq->oh", select_offset.astype(bf16), rel_parts, preferred_element_type=f32
        )
        rel_grad = rel_grad.reshape(REL, 3, HEADS).sum(axis=1)
        table_grad = jnp.dot(select_row.T, rel_grad, precision=highest)
        return jnp.concatenate([sums.reshape(-1), table_grad.reshape(-1)]) * grad_scale

    if exact:

        def add(a, b):
            return (a.astype(f32) + b.astype(f32)).astype(bf16)

        from_far = [swap(grads[4 * color], core) for color in range(3)]
        from_near = [swap(grads[4 * color + 1], core) for color in range(3)]
        far = [add(grads[4 * color + 2], from_far[color]) for color in range(3)]
        small_grad = small_sums(sums, rel_sum, rel_index)
        near = [add(grads[4 * color + 3], from_near[color]) for color in range(3)]
        for stage in range(3):
            for color in range(3):
                received = swap(far[color], orders[color][stage])
                size = received.shape[0] // 2
                far[color] = add(near[color][size:], received[size:])
                near[color] = add(near[color][:size], received[:size])
        parts = [jnp.concatenate(near), swap(jnp.concatenate(far), top)]
        for bit in bits:
            small_grad = small_grad + swap(small_grad, bit)
        owned_grad, new_matrices, new_matrix_m, new_matrix_v = adam_shard(
            kinds, parts, matrices, matrix_m, matrix_v, grad_scale
        )
    else:
        flat_grad = from_pieces(grads[0].astype(f32)) * grad_scale
        owned_grad = lax.psum_scatter(flat_grad, AXES, scatter_dimension=0, tiled=True)
        new_matrices, new_matrix_m, new_matrix_v = adam_step(
            matrices, matrix_m, matrix_v, owned_grad, rate_matrix, decay_rate
        )
        small_grad = lax.psum(small_sums(sums, rel_sum, rel_index), AXES)
    new_small, new_small_m, new_small_v = adam_step(
        small, small_m, small_v, small_grad, rate_small, 0.0
    )
    return (
        output,
        input_grad,
        owned_grad,
        small_grad,
        new_matrices,
        new_matrix_m,
        new_matrix_v,
        new_small,
        new_small_m,
        new_small_v,
    )


def solution(mesh):
    tokens = P(AXES, None, None, None)
    shard = P(AXES)
    whole = P()

    return jax.shard_map(
        on_device,
        mesh=mesh,
        in_specs=(tokens, tokens, whole, whole, shard, shard, shard, whole, whole, whole),
        out_specs=(tokens, tokens, shard, whole, shard, shard, shard, whole, whole, whole),
        check_vma=False,
    )
```

```python
import math

import jax
import jax.numpy as jnp
import numpy as np
from jax import lax
from jax.experimental import pallas as pl
from jax.experimental.pallas import tpu as pltpu
from jax.sharding import PartitionSpec as P


D = 512
HEADS = 16
FF = 2048
WIN = 7
SIDE = 14
SHIFT = 3
STEP = 5
HEAD_DIM = 32
REL = 169

norm_eps = 1e-05
beta_one = 0.9
beta_two = 0.999
adam_eps = 1e-08
rate_matrix = 0.01
rate_small = 0.2
decay_rate = 0.05
masked_score = -1e30
root_half = 0.7071067811865476
inv_root_twopi = 0.3989422804014327
highest = lax.Precision.HIGHEST
score_scale = HEAD_DIM ** (-0.5)

PLACES = WIN * WIN
PAD = 64
WINDOWS = (SIDE // WIN) ** 2
ROWS = WINDOWS * PAD
STRIP = 16
FLAT = SIDE * STRIP
GROUP = 4
GROUPS = HEADS // GROUP
LANES = GROUP * HEAD_DIM
WIDE = GROUP * PAD

PIECE = 64
UP_ROWS = PIECE // (FF // D)
BLOCKS = (3 * D * D + D * D + 2 * D * FF) // (PIECE * D)
QKV_END = 3 * D // PIECE
PROJ_END = QKV_END + D // PIECE
UP_END = PROJ_END + FF // PIECE
SMALL_ROWS = 8 + FF // D
f32 = jnp.float32
bf16 = jnp.bfloat16


def window_source():
    source = np.full((ROWS,), -1, np.int64)
    blocks = SIDE // WIN
    for window in range(WINDOWS):
        for place in range(PLACES):
            row = (window // blocks * WIN + place // WIN + SHIFT) % SIDE
            col = (window % blocks * WIN + place % WIN + SHIFT) % SIDE
            source[window * PAD + place] = row * STRIP + col
    return source


def permutation():
    return (window_source()[:, None] == np.arange(FLAT)[None, :]).astype(np.float32)


def dot(a, b):
    return lax.dot_general(a, b, (((1,), (0,)), ((), ())), preferred_element_type=f32)


def dot_t(a, b):
    return lax.dot_general(a, b, (((1,), (1,)), ((), ())), preferred_element_type=f32)


def t_dot(a, b):
    return lax.dot_general(a, b, (((0,), (0,)), ((), ())), preferred_element_type=f32)


def norm_stats(values):
    center = values - jnp.mean(values, axis=-1, keepdims=True)
    spread = jnp.mean(center * center, axis=-1, keepdims=True)
    scaling = lax.rsqrt(spread + norm_eps)
    return center * scaling, scaling


def norm_back(incoming, normed, scaling, gain_vector):
    scaled = incoming * gain_vector
    return scaling * (
        scaled
        - jnp.mean(scaled, axis=-1, keepdims=True)
        - normed * jnp.mean(scaled * normed, axis=-1, keepdims=True)
    )


def col_sum(values):
    return jnp.sum(values, axis=0, keepdims=True)


def layer_kernel(counts, out_counts):
    n_in = len(counts)
    n_out = len(out_counts)

    def body(*refs):
        slots, out_slots = refs[0], refs[1]
        img, cot, perm, small, bias, mask = refs[2:8]
        pieces = refs[8 : 8 + n_in]
        refs = refs[8 + n_in :]
        out, in_grad, sums, rel_sum = refs[:4]
        grads = refs[4 : 4 + n_out]
        (
            weights,
            wgrad,
            n_one,
            n_two,
            s_one,
            s_two,
            flat,
            xw,
            cw,
            in_one,
            qkv,
            att,
            att_low,
            mixed,
            resid,
            in_two,
            act,
            acc,
            acc_two,
            pre,
            gres,
            grow,
            mgrad,
            dqkv,
            ext,
            sem,
            sem_out,
        ) = refs[4 + n_out :]

        base = 0
        for number, count in enumerate(counts):

            def fetch(slot, carry, number=number, base=base):
                pltpu.make_async_copy(
                    pieces[number].at[slot], weights.at[slots[base + slot]], sem
                ).start()
                return carry

            lax.fori_loop(0, count, fetch, 0, unroll=min(count, 8))
            base += count

        def third_rows(first, count, stride=1):
            parts = [weights[first + stride * number] for number in range(count)]
            return jnp.concatenate(parts, axis=0)

        def qkv_block(part):
            return third_rows(part, D // PIECE, 3)

        def proj_block():
            return weights[QKV_END:PROJ_END].reshape(D, D)

        def up_block(j):
            at = pl.ds(pl.multiple_of(j * UP_ROWS, UP_ROWS), UP_ROWS)
            return weights[PROJ_END:UP_END, at, :].reshape(D, D)

        def down_block(j):
            return weights[pl.ds(UP_END + j * (D // PIECE), D // PIECE)].reshape(D, D)

        gain_one, gain_two, shift_one, bias_query, bias_value, bias_proj, shift_two, bias_down = (
            small[number : number + 1, :] for number in range(8)
        )

        flat[...] = jnp.zeros_like(flat)
        for row in range(SIDE):
            flat[row * STRIP : row * STRIP + SIDE, :] = img[0, row]
        xw[...] = dot(perm[...], flat[...])
        for row in range(SIDE):
            flat[row * STRIP : row * STRIP + SIDE, :] = cot[0, row]
        cw[...] = dot(perm[...], flat[...]).astype(bf16)

        def rows_of(number, size):
            return pl.ds(pl.multiple_of(number * size, size), size)

        def norm_one(number, carry):
            at = rows_of(number, PAD)
            normed, scaling = norm_stats(xw[at, :])
            n_one[at, :] = normed
            s_one[at, :] = jnp.broadcast_to(scaling, (PAD, 128))
            in_one[at, :] = (normed * gain_one + shift_one).astype(bf16)
            return carry

        lax.fori_loop(0, WINDOWS, norm_one, 0, unroll=True)

        for window in range(WINDOWS):
            allowed = mask[window] != 0
            for group in range(GROUPS):
                ext[window, group] = jnp.where(
                    allowed, bias[:, group * WIDE : (group + 1) * WIDE], masked_score
                )
        head_mask = (
            lax.broadcasted_iota(jnp.int32, (WIDE, LANES), 0) // PAD
            == lax.broadcasted_iota(jnp.int32, (WIDE, LANES), 1) // HEAD_DIM
        )

        def spread_heads(values):
            return jnp.where(head_mask, jnp.concatenate([values] * GROUP, axis=0), 0)

        def join_heads(values):
            kept = jnp.where(head_mask, values, 0.0)
            total = kept[:PAD]
            for head in range(1, GROUP):
                total = total + kept[head * PAD : (head + 1) * PAD]
            return total

        pltpu.make_async_copy(weights, weights, sem).wait()

        for part, vector in enumerate((bias_query, None, bias_value)):
            product = dot(in_one[...], qkv_block(part))
            if vector is not None:
                product = product + vector
            qkv[part] = product.astype(bf16)

        def attend(window, carry):
            at = rows_of(window, PAD)
            for group in range(GROUPS):
                lanes = slice(group * LANES, (group + 1) * LANES)
                scores = dot_t(qkv[1, at, lanes], spread_heads(qkv[0, at, lanes]))
                masked = score_scale * scores + ext[window, group]
                top = jnp.max(masked, axis=0, keepdims=True)
                raised = jnp.exp(masked - top)
                attention = raised * (1.0 / col_sum(raised))
                low = attention.astype(bf16)
                att[window, group] = attention
                att_low[window, group] = low
                mixed[at, lanes] = join_heads(t_dot(low, qkv[2, at, lanes])).astype(bf16)
            return carry

        lax.fori_loop(0, WINDOWS, attend, 0, unroll=True)

        resid[...] = xw[...] + (dot(mixed[...], proj_block()) + bias_proj)

        def norm_two(number, carry):
            at = rows_of(number, PAD)
            normed, scaling = norm_stats(resid[at, :])
            n_two[at, :] = normed
            s_two[at, :] = jnp.broadcast_to(scaling, (PAD, 128))
            in_two[at, :] = (normed * gain_two + shift_two).astype(bf16)
            return carry

        lax.fori_loop(0, WINDOWS, norm_two, 0, unroll=True)

        def feed(j, carry):
            acc_two[...] = dot(in_two[...], up_block(j)) + small[pl.ds(8 + j, 1), :]
            pre[...] = dot_t(cw[...], down_block(j))

            def gelu_part(number, total):
                at = rows_of(number, 32)
                value = acc_two[at, :]
                phi = 0.5 * (1.0 + lax.erf(value * root_half))
                act[at, :] = (value * phi).astype(bf16)
                slope = phi + value * jnp.exp(-0.5 * value * value) * inv_root_twopi
                back = pre[at, :] * slope
                grow[at, :] = back.astype(bf16)
                return total + col_sum(back)

            sums[pl.ds(8 + j, 1), :] = lax.fori_loop(
                0, ROWS // 32, gelu_part, jnp.zeros((1, D), f32), unroll=True
            )
            forward = dot(act[...], down_block(j))
            backward = dot_t(grow[...], up_block(j))

            @pl.when(j == 0)
            def _():
                acc[...] = forward
                gres[...] = backward

            @pl.when(j > 0)
            def _():
                acc[...] += forward
                gres[...] += backward

            up_grad = t_dot(in_two[...], grow[...]).astype(bf16)
            at = pl.ds(pl.multiple_of(j * UP_ROWS, UP_ROWS), UP_ROWS)
            wgrad[PROJ_END:UP_END, at, :] = up_grad.reshape(FF // PIECE, UP_ROWS, D)
            down_grad = t_dot(act[...], cw[...]).astype(bf16)
            wgrad[pl.ds(UP_END + j * (D // PIECE), D // PIECE)] = down_grad.reshape(
                D // PIECE, PIECE, D
            )
            return carry

        lax.fori_loop(0, FF // D, feed, 0, unroll=True)

        def second_back(number, carry):
            gain_sum, shift_sum, resid_sum, cot_sum = carry
            at = rows_of(number, 32)
            value = resid[at, :]
            normed, scaling = n_two[at, :], s_two[at, 0:1]
            act[at, :] = (value + (acc[at, :] + bias_down)).astype(bf16)
            incoming = gres[at, :]
            back = norm_back(incoming, normed, scaling, gain_two)
            cotangent = cw[at, :].astype(f32)
            total = cotangent + back
            gres[at, :] = total
            grow[at, :] = total.astype(bf16)
            return (
                gain_sum + col_sum(incoming * normed),
                shift_sum + col_sum(incoming),
                resid_sum + col_sum(total),
                cot_sum + col_sum(cotangent),
            )

        zero_row = jnp.zeros((1, D), f32)
        sums[1:2, :], sums[6:7, :], sums[5:6, :], sums[7:8, :] = lax.fori_loop(
            0, ROWS // 32, second_back, (zero_row,) * 4, unroll=True
        )
        result = t_dot(perm[...], act[...]).astype(bf16)
        for row in range(SIDE):
            out[0, row] = result[row * STRIP : row * STRIP + SIDE, :]

        proj_grad = t_dot(mixed[...], grow[...]).astype(bf16)
        wgrad[QKV_END:PROJ_END] = proj_grad.reshape(D // PIECE, PIECE, D)
        mgrad[...] = dot_t(grow[...], proj_block()).astype(bf16)
        sums[3:4, :] = zero_row
        sums[4:5, :] = zero_row
        rel_sum[...] = jnp.zeros_like(rel_sum)

        def attend_back(window, carry):
            at = rows_of(window, PAD)
            for group in range(GROUPS):
                lanes = slice(group * LANES, (group + 1) * LANES)
                wide = slice(group * WIDE, (group + 1) * WIDE)
                mixed_blk = spread_heads(mgrad[at, lanes])
                query_blk = spread_heads(qkv[0, at, lanes])
                prob = dot_t(qkv[2, at, lanes], mixed_blk)
                attention = att[window, group]
                score = attention * (prob - col_sum(attention * prob))
                rel_sum[:, wide] += score
                low = score.astype(bf16)
                value_grad = dot(att_low[window, group], mixed_blk)
                key_grad = score_scale * dot(low, query_blk)
                query_grad = score_scale * join_heads(t_dot(low, qkv[1, at, lanes]))
                sums[3:4, lanes] += col_sum(query_grad)
                sums[4:5, lanes] += col_sum(value_grad)
                dqkv[0, at, lanes] = query_grad.astype(bf16)
                dqkv[1, at, lanes] = key_grad.astype(bf16)
                dqkv[2, at, lanes] = value_grad.astype(bf16)
            return carry

        lax.fori_loop(0, WINDOWS, attend_back, 0, unroll=True)

        for part in range(3):
            part_grad = t_dot(in_one[...], dqkv[part]).astype(bf16)
            for number in range(D // PIECE):
                wgrad[3 * number + part] = part_grad[number * PIECE : (number + 1) * PIECE]

        base = 0
        for number, count in enumerate(out_counts):

            def store(slot, carry, number=number, base=base):
                pltpu.make_async_copy(
                    wgrad.at[out_slots[base + slot]], grads[number].at[slot], sem_out
                ).start()
                return carry

            lax.fori_loop(0, count, store, 0, unroll=min(count, 8))
            base += count

        acc[...] = (
            dot_t(dqkv[0], qkv_block(0)) + dot_t(dqkv[1], qkv_block(1))
        ) + dot_t(dqkv[2], qkv_block(2))

        def first_back(number, carry):
            gain_sum, shift_sum = carry
            at = rows_of(number, 32)
            normed, scaling = n_one[at, :], s_one[at, 0:1]
            incoming = acc[at, :]
            back = norm_back(incoming, normed, scaling, gain_one)
            act[at, :] = (gres[at, :] + back).astype(bf16)
            return gain_sum + col_sum(incoming * normed), shift_sum + col_sum(incoming)

        sums[0:1, :], sums[2:3, :] = lax.fori_loop(
            0, ROWS // 32, first_back, (zero_row,) * 2, unroll=True
        )
        result = t_dot(perm[...], act[...]).astype(bf16)
        for row in range(SIDE):
            in_grad[0, row] = result[row * STRIP : row * STRIP + SIDE, :]
        pltpu.make_async_copy(wgrad, wgrad, sem_out).wait()

    return body


def run_layer(images, cotangent, small, bias, mask, slots, out_slots, pieces, outs):
    perm = jnp.asarray(permutation(), bf16)
    vmem = pl.BlockSpec(memory_space=pltpu.VMEM)
    smem = pl.BlockSpec(memory_space=pltpu.SMEM)
    hbm = pl.BlockSpec(memory_space=pl.ANY)
    counts = [piece.shape[0] for piece in pieces]
    image_shape = (1, SIDE, SIDE, D)
    return pl.pallas_call(
        layer_kernel(counts, outs),
        in_specs=[smem, smem] + [vmem] * 6 + [hbm] * len(counts),
        out_specs=[vmem] * 4 + [hbm] * len(outs),
        out_shape=[
            jax.ShapeDtypeStruct(image_shape, bf16),
            jax.ShapeDtypeStruct(image_shape, bf16),
            jax.ShapeDtypeStruct((SMALL_ROWS, D), f32),
            jax.ShapeDtypeStruct((PAD, HEADS * PAD), f32),
        ]
        + [jax.ShapeDtypeStruct((count, PIECE, D), bf16) for count in outs],
        scratch_shapes=[
            pltpu.VMEM((BLOCKS, PIECE, D), bf16),
            pltpu.VMEM((BLOCKS, PIECE, D), bf16),
            pltpu.VMEM((ROWS, D), f32),
            pltpu.VMEM((ROWS, D), f32),
            pltpu.VMEM((ROWS, 128), f32),
            pltpu.VMEM((ROWS, 128), f32),
            pltpu.VMEM((FLAT, D), bf16),
            pltpu.VMEM((ROWS, D), f32),
            pltpu.VMEM((ROWS, D), bf16),
            pltpu.VMEM((ROWS, D), bf16),
            pltpu.VMEM((3, ROWS, D), bf16),
            pltpu.VMEM((WINDOWS, GROUPS, PAD, WIDE), f32),
            pltpu.VMEM((WINDOWS, GROUPS, PAD, WIDE), bf16),
            pltpu.VMEM((ROWS, D), bf16),
            pltpu.VMEM((ROWS, D), f32),
            pltpu.VMEM((ROWS, D), bf16),
            pltpu.VMEM((ROWS, D), bf16),
            pltpu.VMEM((ROWS, D), f32),
            pltpu.VMEM((ROWS, D), f32),
            pltpu.VMEM((ROWS, D), f32),
            pltpu.VMEM((ROWS, D), f32),
            pltpu.VMEM((ROWS, D), bf16),
            pltpu.VMEM((ROWS, D), bf16),
            pltpu.VMEM((3, ROWS, D), bf16),
            pltpu.VMEM((WINDOWS, GROUPS, PAD, WIDE), f32),
            pltpu.SemaphoreType.DMA,
            pltpu.SemaphoreType.DMA,
        ],
        name="layer",
    )(slots, out_slots, images, cotangent, perm, small, bias, mask, *pieces)


VIEW = PIECE * D * 3 // 128


def shard_kinds(device):
    third = 3 * device + jnp.arange(3, dtype=jnp.int32)
    is_up = (third >= PROJ_END) & (third < UP_END)
    return jnp.where(third < QKV_END, 0, jnp.where(is_up, 2, 1)).astype(jnp.int32)


def piece_rows(kind, part):
    per_row = D // 128
    if kind == 0:
        return [(slice(0, PIECE), per_row * part, 3 * per_row)]
    if kind == 1:
        return [(slice(0, PIECE), per_row * PIECE * part, per_row)]
    return [
        (slice(j * UP_ROWS, (j + 1) * UP_ROWS), per_row * (PIECE * part + j), per_row * (FF // D))
        for j in range(FF // D)
    ]


def pack_kernel(kinds, shard, out):
    for part in range(3):
        for kind in range(3):

            @pl.when(kinds[part] == kind)
            def _(part=part, kind=kind):
                for rows, start, stride in piece_rows(kind, part):
                    size = rows.stop - rows.start
                    for lane in range(D // 128):
                        lanes = slice(lane * 128, (lane + 1) * 128)
                        value = shard[pl.ds(start + lane, size, stride=stride), :].astype(bf16)
                        out[part, rows, lanes] = value


def pack_shard(shard, kinds):
    vmem = pl.BlockSpec(memory_space=pltpu.VMEM)
    return pl.pallas_call(
        pack_kernel,
        in_specs=[pl.BlockSpec(memory_space=pltpu.SMEM), vmem],
        out_specs=vmem,
        out_shape=jax.ShapeDtypeStruct((3, PIECE, D), bf16),
        name="pack",
    )(kinds, shard.reshape(VIEW, 128))


def adam_step(weights, first_moment, second_moment, gradient, rate, decay):
    new_first = beta_one * first_moment + (1.0 - beta_one) * gradient
    new_second = beta_two * second_moment + (1.0 - beta_two) * gradient * gradient
    first_hat = new_first / (1.0 - beta_one**STEP)
    second_hat = new_second / (1.0 - beta_two**STEP)
    update = first_hat / (jnp.sqrt(second_hat) + adam_eps) + decay * weights
    return (weights - rate * update, new_first, new_second)


def adam_kernel(grad_scale):
    def body(kinds, *refs):
        mine, theirs, weights, first, second = refs[:5]
        grad, new_weights, new_first, new_second = refs[5:9]
        for part in range(3):
            for kind in range(3):

                @pl.when(kinds[part] == kind)
                def _(part=part, kind=kind):
                    for rows, start, stride in piece_rows(kind, part):
                        size = rows.stop - rows.start
                        for lane in range(D // 128):
                            lanes = slice(lane * 128, (lane + 1) * 128)
                            total = mine[part, rows, lanes].astype(f32) + theirs[
                                part, rows, lanes
                            ].astype(f32)
                            grad[pl.ds(start + lane, size, stride=stride), :] = total * grad_scale

        def step(number, carry):
            at = pl.ds(pl.multiple_of(number * 64, 64), 64)
            new_weights[at, :], new_first[at, :], new_second[at, :] = adam_step(
                weights[at, :], first[at, :], second[at, :], grad[at, :], rate_matrix, decay_rate
            )
            return carry

        lax.fori_loop(0, VIEW // 64, step, 0)

    return body


def adam_shard(kinds, parts, weights, first, second, grad_scale):
    vmem = pl.BlockSpec(memory_space=pltpu.VMEM)
    size = weights.shape[0]
    results = pl.pallas_call(
        adam_kernel(grad_scale),
        in_specs=[pl.BlockSpec(memory_space=pltpu.SMEM)] + [vmem] * 5,
        out_specs=[vmem] * 4,
        out_shape=[jax.ShapeDtypeStruct((VIEW, 128), f32)] * 4,
        name="adam",
    )(kinds, *parts, *(array.reshape(VIEW, 128) for array in (weights, first, second)))
    return [result.reshape(size) for result in results]


def to_pieces(flat):
    q_end, p_end, u_end = QKV_END * PIECE * D, PROJ_END * PIECE * D, UP_END * PIECE * D
    qkv = flat[:q_end].reshape(-1, PIECE, 3, D).transpose(0, 2, 1, 3).reshape(-1, PIECE, D)
    proj = flat[q_end:p_end].reshape(-1, PIECE, D)
    up = flat[p_end:u_end].reshape(-1, UP_ROWS, FF // D, D).transpose(0, 2, 1, 3)
    down = flat[u_end:].reshape(-1, PIECE, D)
    return jnp.concatenate([qkv, proj, up.reshape(-1, PIECE, D), down])


def from_pieces(pieces):
    qkv = pieces[:QKV_END].reshape(-1, 3, PIECE, D).transpose(0, 2, 1, 3)
    up = pieces[PROJ_END:UP_END].reshape(-1, FF // D, UP_ROWS, D).transpose(0, 2, 1, 3)
    return jnp.concatenate(
        [
            qkv.reshape(-1),
            pieces[QKV_END:PROJ_END].reshape(-1),
            up.reshape(-1),
            pieces[UP_END:].reshape(-1),
        ]
    )


def offset_grid():
    spots = np.arange(PAD)
    rows_at = spots // WIN
    cols_at = spots % WIN
    grid = (rows_at[None, :] - rows_at[:, None] + WIN - 1) * (2 * WIN - 1) + (
        cols_at[None, :] - cols_at[:, None] + WIN - 1
    )
    real = (spots[:, None] < PLACES) & (spots[None, :] < PLACES)
    return np.where(real, grid, -1)


AXES = ("rep", "grp")


def on_device(
    images, cotangent, region_ids, rel_index, matrices, matrix_m, matrix_v, small, small_m, small_v
):
    devices = lax.axis_size("rep") * lax.axis_size("grp")
    me = lax.axis_index(AXES)
    bits = [1 << number for number in range(devices.bit_length() - 1)]
    exact = devices == sum(bits) + 1 and matrices.shape[0] == 3 * PIECE * D

    def swap(value, bit):
        return lax.ppermute(value, AXES, [(i, i ^ bit) for i in range(devices)])

    labels = jnp.arange(REL, dtype=jnp.int32)
    grid = jnp.asarray(offset_grid(), jnp.int32)

    def split(values):
        high = lax.reduce_precision(values, 8, 7)
        middle = lax.reduce_precision(values - high, 8, 7)
        low = values - high - middle
        return [part.astype(bf16) for part in (high, middle, low)]

    def tables(rel_index):
        select_offset = (grid[None] == labels[:, None, None]).astype(f32)
        select_row = (rel_index[:, None] == labels[None, :]).astype(f32)
        return select_offset, select_row

    def prepare(small, region_ids, rel_index):
        small_rows = small[: SMALL_ROWS * D].reshape(SMALL_ROWS, D)
        rel_table = small[SMALL_ROWS * D :].reshape(REL, HEADS)
        select_offset, select_row = tables(rel_index)
        table_rows = jnp.dot(select_row, rel_table, precision=highest)
        table_parts = jnp.concatenate(split(table_rows), axis=1)
        bias = jnp.einsum(
            "okq,oh->khq", select_offset.astype(bf16), table_parts, preferred_element_type=f32
        )
        bias = bias.reshape(PAD, 3, HEADS, PAD).sum(axis=1)
        blocks = SIDE // WIN
        regions = region_ids.reshape(blocks, WIN, blocks, WIN).transpose(0, 2, 1, 3)
        regions = regions.reshape(WINDOWS, PLACES)
        padded = ((0, 0), (0, PAD - PLACES))
        keys = jnp.pad(regions, padded, constant_values=-1)[:, :, None]
        queries = jnp.tile(jnp.pad(regions, padded, constant_values=-2), (1, GROUP))[:, None, :]
        mask = (keys == queries).astype(jnp.int32)
        return small_rows, bias.reshape(PAD, HEADS * PAD), mask

    if exact:
        core, inner, top = bits[0], bits[1:-1], bits[-1]
        orders = [inner[color:] + inner[:color] for color in range(3)]
        kinds = shard_kinds(me)
        packed = pack_shard(matrices, kinds)
        received = swap(packed, top)
        masks = [[0]] * 3 + [[top]] * 3
        for color in range(3):
            for step in range(1, len(inner)):
                for at in (color, 3 + color):
                    bit = orders[color][-step]
                    masks[at] = masks[at] + [mask ^ bit for mask in masks[at]]

        def slot_table(entries):
            table = jnp.asarray(entries, jnp.int32)
            return 3 * (me ^ table[:, 0]) + table[:, 1]

        out_entries = []
        for color in range(3):
            order = orders[color] + [top]
            half = [0]
            for bit in reversed(order[1:]):
                half = half + [mask ^ bit for mask in half]
            for extra in (order[0] ^ core, core, order[0], 0):
                out_entries += [(mask ^ extra, color) for mask in half]
        piece_entries = []
        for tree in range(2):
            for color in range(3):
                last = orders[color][0]
                for extra in (0, last, core, last ^ core):
                    piece_entries += [(mask ^ extra, color) for mask in masks[3 * tree + color]]
        operands = prepare(small, region_ids, rel_index)
        operands = (*operands, slot_table(piece_entries), slot_table(out_entries))
        received, operands = lax.optimization_barrier((received, operands))
        buffers = [tree[color : color + 1] for tree in (packed, received) for color in range(3)]
        for step, tree in ((1, 0), (1, 1), (2, 0), (2, 1)):
            for color in range(3):
                at = 3 * tree + color
                bit = orders[color][-step]
                own = buffers[at]
                other = swap(own, bit)
                buffers[at] = jnp.concatenate([own, other])

        pieces = []
        for tree in range(2):
            for color in range(3):
                buffer = buffers[3 * tree + color]
                far = swap(buffer, orders[color][0])
                pieces += [buffer, far, swap(buffer, core), swap(far, core)]
        outs = [devices // 4] * 12
    else:
        gathered = lax.all_gather(matrices.astype(bf16), AXES, axis=0, tiled=True)
        pieces = [to_pieces(gathered)]
        slots = jnp.arange(BLOCKS, dtype=jnp.int32)
        operands = (*prepare(small, region_ids, rel_index), slots, slots)
        outs = [BLOCKS]

    output, input_grad, sums, rel_sum, *grads = run_layer(
        images, cotangent, *operands, pieces, outs
    )

    tokens_all = images.shape[0] * devices * SIDE * SIDE
    grad_scale = 1.0 / math.sqrt(tokens_all)

    def small_sums(sums, rel_sum, rel_index):
        select_offset, select_row = tables(rel_index)
        rel_parts = jnp.concatenate(split(rel_sum.reshape(PAD, HEADS, PAD)), axis=1)
        rel_grad = jnp.einsum(
            "okq,khq->oh", select_offset.astype(bf16), rel_parts, preferred_element_type=f32
        )
        rel_grad = rel_grad.reshape(REL, 3, HEADS).sum(axis=1)
        table_grad = jnp.dot(select_row.T, rel_grad, precision=highest)
        return jnp.concatenate([sums.reshape(-1), table_grad.reshape(-1)]) * grad_scale

    if exact:

        def add(a, b):
            return (a.astype(f32) + b.astype(f32)).astype(bf16)

        from_far = [swap(grads[4 * color], core) for color in range(3)]
        from_near = [swap(grads[4 * color + 1], core) for color in range(3)]
        far = [add(grads[4 * color + 2], from_far[color]) for color in range(3)]
        small_grad = small_sums(sums, rel_sum, rel_index)
        near = [add(grads[4 * color + 3], from_near[color]) for color in range(3)]
        for stage in range(3):
            for color in range(3):
                received = swap(far[color], orders[color][stage])
                size = received.shape[0] // 2
                far[color] = add(near[color][size:], received[size:])
                near[color] = add(near[color][:size], received[:size])
        parts = [jnp.concatenate(near), swap(jnp.concatenate(far), top)]
        for bit in bits:
            small_grad = small_grad + swap(small_grad, bit)
        parts = [pltpu.with_memory_space_constraint(piece, pltpu.VMEM) for piece in parts]
        owned_grad, new_matrices, new_matrix_m, new_matrix_v = adam_shard(
            kinds, parts, matrices, matrix_m, matrix_v, grad_scale
        )
    else:
        flat_grad = from_pieces(grads[0].astype(f32)) * grad_scale
        owned_grad = lax.psum_scatter(flat_grad, AXES, scatter_dimension=0, tiled=True)
        new_matrices, new_matrix_m, new_matrix_v = adam_step(
            matrices, matrix_m, matrix_v, owned_grad, rate_matrix, decay_rate
        )
        small_grad = lax.psum(small_sums(sums, rel_sum, rel_index), AXES)
    new_small, new_small_m, new_small_v = adam_step(
        small, small_m, small_v, small_grad, rate_small, 0.0
    )
    return (
        output,
        input_grad,
        owned_grad,
        small_grad,
        new_matrices,
        new_matrix_m,
        new_matrix_v,
        new_small,
        new_small_m,
        new_small_v,
    )


def solution(mesh):
    tokens = P(AXES, None, None, None)
    shard = P(AXES)
    whole = P()

    return jax.shard_map(
        on_device,
        mesh=mesh,
        in_specs=(tokens, tokens, whole, whole, shard, shard, shard, whole, whole, whole),
        out_specs=(tokens, tokens, shard, whole, shard, shard, shard, whole, whole, whole),
        check_vma=False,
    )
```

```python
import math

import jax
import jax.numpy as jnp
import numpy as np
from jax import lax
from jax.experimental import pallas as pl
from jax.experimental.pallas import tpu as pltpu
from jax.sharding import PartitionSpec as P


D = 512
HEADS = 16
FF = 2048
WIN = 7
SIDE = 14
SHIFT = 3
STEP = 5
HEAD_DIM = 32
REL = 169

norm_eps = 1e-05
beta_one = 0.9
beta_two = 0.999
adam_eps = 1e-08
rate_matrix = 0.01
rate_small = 0.2
decay_rate = 0.05
masked_score = -1e30
root_half = 0.7071067811865476
inv_root_twopi = 0.3989422804014327
highest = lax.Precision.HIGHEST
score_scale = HEAD_DIM ** (-0.5)

PLACES = WIN * WIN
PAD = 64
WINDOWS = (SIDE // WIN) ** 2
ROWS = WINDOWS * PAD
STRIP = 16
FLAT = SIDE * STRIP
GROUP = 4
GROUPS = HEADS // GROUP
LANES = GROUP * HEAD_DIM
WIDE = GROUP * PAD

PIECE = 64
UP_ROWS = PIECE // (FF // D)
BLOCKS = (3 * D * D + D * D + 2 * D * FF) // (PIECE * D)
QKV_END = 3 * D // PIECE
PROJ_END = QKV_END + D // PIECE
UP_END = PROJ_END + FF // PIECE
SMALL_ROWS = 8 + FF // D
f32 = jnp.float32
bf16 = jnp.bfloat16


def window_source():
    source = np.full((ROWS,), -1, np.int64)
    blocks = SIDE // WIN
    for window in range(WINDOWS):
        for place in range(PLACES):
            row = (window // blocks * WIN + place // WIN + SHIFT) % SIDE
            col = (window % blocks * WIN + place % WIN + SHIFT) % SIDE
            source[window * PAD + place] = row * STRIP + col
    return source


def permutation():
    return (window_source()[:, None] == np.arange(FLAT)[None, :]).astype(np.float32)


def dot(a, b):
    return lax.dot_general(a, b, (((1,), (0,)), ((), ())), preferred_element_type=f32)


def dot_t(a, b):
    return lax.dot_general(a, b, (((1,), (1,)), ((), ())), preferred_element_type=f32)


def t_dot(a, b):
    return lax.dot_general(a, b, (((0,), (0,)), ((), ())), preferred_element_type=f32)


def norm_stats(values):
    center = values - jnp.mean(values, axis=-1, keepdims=True)
    spread = jnp.mean(center * center, axis=-1, keepdims=True)
    scaling = lax.rsqrt(spread + norm_eps)
    return center * scaling, scaling


def norm_back(incoming, normed, scaling, gain_vector):
    scaled = incoming * gain_vector
    return scaling * (
        scaled
        - jnp.mean(scaled, axis=-1, keepdims=True)
        - normed * jnp.mean(scaled * normed, axis=-1, keepdims=True)
    )


def col_sum(values):
    return jnp.sum(values, axis=0, keepdims=True)


def layer_kernel(counts, out_counts):
    n_in = len(counts)
    n_out = len(out_counts)

    def body(*refs):
        slots, out_slots = refs[0], refs[1]
        img, cot, perm, small, bias, mask = refs[2:8]
        pieces = refs[8 : 8 + n_in]
        refs = refs[8 + n_in :]
        out, in_grad, sums, rel_sum = refs[:4]
        grads = refs[4 : 4 + n_out]
        (
            weights,
            wgrad,
            n_one,
            n_two,
            s_one,
            s_two,
            flat,
            xw,
            cw,
            in_one,
            qkv,
            att,
            att_low,
            mixed,
            resid,
            in_two,
            act,
            acc,
            acc_two,
            pre,
            gres,
            grow,
            mgrad,
            dqkv,
            ext,
            sem,
            sem_out,
        ) = refs[4 + n_out :]

        base = 0
        for number, count in enumerate(counts):

            def fetch(slot, carry, number=number, base=base):
                pltpu.make_async_copy(
                    pieces[number].at[slot], weights.at[slots[base + slot]], sem
                ).start()
                return carry

            lax.fori_loop(0, count, fetch, 0, unroll=min(count, 8))
            base += count

        def third_rows(first, count, stride=1):
            parts = [weights[first + stride * number] for number in range(count)]
            return jnp.concatenate(parts, axis=0)

        def qkv_block(part):
            return third_rows(part, D // PIECE, 3)

        def proj_block():
            return weights[QKV_END:PROJ_END].reshape(D, D)

        def up_block(j):
            at = pl.ds(pl.multiple_of(j * UP_ROWS, UP_ROWS), UP_ROWS)
            return weights[PROJ_END:UP_END, at, :].reshape(D, D)

        def down_block(j):
            return weights[pl.ds(UP_END + j * (D // PIECE), D // PIECE)].reshape(D, D)

        gain_one, gain_two, shift_one, bias_query, bias_value, bias_proj, shift_two, bias_down = (
            small[number : number + 1, :] for number in range(8)
        )

        flat[...] = jnp.zeros_like(flat)
        for row in range(SIDE):
            flat[row * STRIP : row * STRIP + SIDE, :] = img[0, row]
        xw[...] = dot(perm[...], flat[...])
        for row in range(SIDE):
            flat[row * STRIP : row * STRIP + SIDE, :] = cot[0, row]
        cw[...] = dot(perm[...], flat[...]).astype(bf16)

        def rows_of(number, size):
            return pl.ds(pl.multiple_of(number * size, size), size)

        def norm_one(number, carry):
            at = rows_of(number, PAD)
            normed, scaling = norm_stats(xw[at, :])
            n_one[at, :] = normed
            s_one[at, :] = jnp.broadcast_to(scaling, (PAD, 128))
            in_one[at, :] = (normed * gain_one + shift_one).astype(bf16)
            return carry

        lax.fori_loop(0, WINDOWS, norm_one, 0, unroll=True)

        for window in range(WINDOWS):
            allowed = mask[window] != 0
            for group in range(GROUPS):
                ext[window, group] = jnp.where(
                    allowed, bias[:, group * WIDE : (group + 1) * WIDE], masked_score
                )
        head_mask = (
            lax.broadcasted_iota(jnp.int32, (WIDE, LANES), 0) // PAD
            == lax.broadcasted_iota(jnp.int32, (WIDE, LANES), 1) // HEAD_DIM
        )

        def spread_heads(values):
            return jnp.where(head_mask, jnp.concatenate([values] * GROUP, axis=0), 0)

        def join_heads(values):
            kept = jnp.where(head_mask, values, 0.0)
            total = kept[:PAD]
            for head in range(1, GROUP):
                total = total + kept[head * PAD : (head + 1) * PAD]
            return total

        pltpu.make_async_copy(weights, weights, sem).wait()

        for part, vector in enumerate((bias_query, None, bias_value)):
            product = dot(in_one[...], qkv_block(part))
            if vector is not None:
                product = product + vector
            qkv[part] = product.astype(bf16)

        def attend(window, carry):
            at = rows_of(window, PAD)
            for group in range(GROUPS):
                lanes = slice(group * LANES, (group + 1) * LANES)
                scores = dot_t(qkv[1, at, lanes], spread_heads(qkv[0, at, lanes]))
                masked = score_scale * scores + ext[window, group]
                top = jnp.max(masked, axis=0, keepdims=True)
                raised = jnp.exp(masked - top)
                attention = raised * (1.0 / col_sum(raised))
                low = attention.astype(bf16)
                att[window, group] = attention
                att_low[window, group] = low
                mixed[at, lanes] = join_heads(t_dot(low, qkv[2, at, lanes])).astype(bf16)
            return carry

        lax.fori_loop(0, WINDOWS, attend, 0, unroll=True)

        resid[...] = xw[...] + (dot(mixed[...], proj_block()) + bias_proj)

        def norm_two(number, carry):
            at = rows_of(number, PAD)
            normed, scaling = norm_stats(resid[at, :])
            n_two[at, :] = normed
            s_two[at, :] = jnp.broadcast_to(scaling, (PAD, 128))
            in_two[at, :] = (normed * gain_two + shift_two).astype(bf16)
            return carry

        lax.fori_loop(0, WINDOWS, norm_two, 0, unroll=True)

        def feed(j, carry):
            acc_two[...] = dot(in_two[...], up_block(j)) + small[pl.ds(8 + j, 1), :]
            pre[...] = dot_t(cw[...], down_block(j))

            def gelu_part(number, total):
                at = rows_of(number, 32)
                value = acc_two[at, :]
                phi = 0.5 * (1.0 + lax.erf(value * root_half))
                act[at, :] = (value * phi).astype(bf16)
                slope = phi + value * jnp.exp(-0.5 * value * value) * inv_root_twopi
                back = pre[at, :] * slope
                grow[at, :] = back.astype(bf16)
                return total + col_sum(back)

            sums[pl.ds(8 + j, 1), :] = lax.fori_loop(
                0, ROWS // 32, gelu_part, jnp.zeros((1, D), f32), unroll=True
            )
            forward = dot(act[...], down_block(j))
            backward = dot_t(grow[...], up_block(j))

            @pl.when(j == 0)
            def _():
                acc[...] = forward
                gres[...] = backward

            @pl.when(j > 0)
            def _():
                acc[...] += forward
                gres[...] += backward

            up_grad = t_dot(in_two[...], grow[...]).astype(bf16)
            at = pl.ds(pl.multiple_of(j * UP_ROWS, UP_ROWS), UP_ROWS)
            wgrad[PROJ_END:UP_END, at, :] = up_grad.reshape(FF // PIECE, UP_ROWS, D)
            down_grad = t_dot(act[...], cw[...]).astype(bf16)
            wgrad[pl.ds(UP_END + j * (D // PIECE), D // PIECE)] = down_grad.reshape(
                D // PIECE, PIECE, D
            )
            return carry

        lax.fori_loop(0, FF // D, feed, 0, unroll=True)

        def second_back(number, carry):
            gain_sum, shift_sum, resid_sum, cot_sum = carry
            at = rows_of(number, 32)
            value = resid[at, :]
            normed, scaling = n_two[at, :], s_two[at, 0:1]
            act[at, :] = (value + (acc[at, :] + bias_down)).astype(bf16)
            incoming = gres[at, :]
            back = norm_back(incoming, normed, scaling, gain_two)
            cotangent = cw[at, :].astype(f32)
            total = cotangent + back
            gres[at, :] = total
            grow[at, :] = total.astype(bf16)
            return (
                gain_sum + col_sum(incoming * normed),
                shift_sum + col_sum(incoming),
                resid_sum + col_sum(total),
                cot_sum + col_sum(cotangent),
            )

        zero_row = jnp.zeros((1, D), f32)
        sums[1:2, :], sums[6:7, :], sums[5:6, :], sums[7:8, :] = lax.fori_loop(
            0, ROWS // 32, second_back, (zero_row,) * 4, unroll=True
        )
        result = t_dot(perm[...], act[...]).astype(bf16)
        for row in range(SIDE):
            out[0, row] = result[row * STRIP : row * STRIP + SIDE, :]

        proj_grad = t_dot(mixed[...], grow[...]).astype(bf16)
        wgrad[QKV_END:PROJ_END] = proj_grad.reshape(D // PIECE, PIECE, D)
        mgrad[...] = dot_t(grow[...], proj_block()).astype(bf16)
        sums[3:4, :] = zero_row
        sums[4:5, :] = zero_row
        rel_sum[...] = jnp.zeros_like(rel_sum)

        def attend_back(window, carry):
            at = rows_of(window, PAD)
            for group in range(GROUPS):
                lanes = slice(group * LANES, (group + 1) * LANES)
                wide = slice(group * WIDE, (group + 1) * WIDE)
                mixed_blk = spread_heads(mgrad[at, lanes])
                query_blk = spread_heads(qkv[0, at, lanes])
                prob = dot_t(qkv[2, at, lanes], mixed_blk)
                attention = att[window, group]
                score = attention * (prob - col_sum(attention * prob))
                rel_sum[:, wide] += score
                low = score.astype(bf16)
                value_grad = dot(att_low[window, group], mixed_blk)
                key_grad = score_scale * dot(low, query_blk)
                query_grad = score_scale * join_heads(t_dot(low, qkv[1, at, lanes]))
                sums[3:4, lanes] += col_sum(query_grad)
                sums[4:5, lanes] += col_sum(value_grad)
                dqkv[0, at, lanes] = query_grad.astype(bf16)
                dqkv[1, at, lanes] = key_grad.astype(bf16)
                dqkv[2, at, lanes] = value_grad.astype(bf16)
            return carry

        lax.fori_loop(0, WINDOWS, attend_back, 0, unroll=True)

        for part in range(3):
            part_grad = t_dot(in_one[...], dqkv[part]).astype(bf16)
            for number in range(D // PIECE):
                wgrad[3 * number + part] = part_grad[number * PIECE : (number + 1) * PIECE]

        base = 0
        for number, count in enumerate(out_counts):

            def store(slot, carry, number=number, base=base):
                pltpu.make_async_copy(
                    wgrad.at[out_slots[base + slot]], grads[number].at[slot], sem_out
                ).start()
                return carry

            lax.fori_loop(0, count, store, 0, unroll=min(count, 8))
            base += count

        acc[...] = (
            dot_t(dqkv[0], qkv_block(0)) + dot_t(dqkv[1], qkv_block(1))
        ) + dot_t(dqkv[2], qkv_block(2))

        def first_back(number, carry):
            gain_sum, shift_sum = carry
            at = rows_of(number, 32)
            normed, scaling = n_one[at, :], s_one[at, 0:1]
            incoming = acc[at, :]
            back = norm_back(incoming, normed, scaling, gain_one)
            act[at, :] = (gres[at, :] + back).astype(bf16)
            return gain_sum + col_sum(incoming * normed), shift_sum + col_sum(incoming)

        sums[0:1, :], sums[2:3, :] = lax.fori_loop(
            0, ROWS // 32, first_back, (zero_row,) * 2, unroll=True
        )
        result = t_dot(perm[...], act[...]).astype(bf16)
        for row in range(SIDE):
            in_grad[0, row] = result[row * STRIP : row * STRIP + SIDE, :]
        pltpu.make_async_copy(wgrad, wgrad, sem_out).wait()

    return body


def run_layer(images, cotangent, small, bias, mask, slots, out_slots, pieces, outs):
    perm = jnp.asarray(permutation(), bf16)
    vmem = pl.BlockSpec(memory_space=pltpu.VMEM)
    smem = pl.BlockSpec(memory_space=pltpu.SMEM)
    hbm = pl.BlockSpec(memory_space=pl.ANY)
    counts = [piece.shape[0] for piece in pieces]
    image_shape = (1, SIDE, SIDE, D)
    return pl.pallas_call(
        layer_kernel(counts, outs),
        in_specs=[smem, smem] + [vmem] * 6 + [hbm] * len(counts),
        out_specs=[vmem] * 4 + [hbm] * len(outs),
        out_shape=[
            jax.ShapeDtypeStruct(image_shape, bf16),
            jax.ShapeDtypeStruct(image_shape, bf16),
            jax.ShapeDtypeStruct((SMALL_ROWS, D), f32),
            jax.ShapeDtypeStruct((PAD, HEADS * PAD), f32),
        ]
        + [jax.ShapeDtypeStruct((count, PIECE, D), bf16) for count in outs],
        scratch_shapes=[
            pltpu.VMEM((BLOCKS, PIECE, D), bf16),
            pltpu.VMEM((BLOCKS, PIECE, D), bf16),
            pltpu.VMEM((ROWS, D), f32),
            pltpu.VMEM((ROWS, D), f32),
            pltpu.VMEM((ROWS, 128), f32),
            pltpu.VMEM((ROWS, 128), f32),
            pltpu.VMEM((FLAT, D), bf16),
            pltpu.VMEM((ROWS, D), f32),
            pltpu.VMEM((ROWS, D), bf16),
            pltpu.VMEM((ROWS, D), bf16),
            pltpu.VMEM((3, ROWS, D), bf16),
            pltpu.VMEM((WINDOWS, GROUPS, PAD, WIDE), f32),
            pltpu.VMEM((WINDOWS, GROUPS, PAD, WIDE), bf16),
            pltpu.VMEM((ROWS, D), bf16),
            pltpu.VMEM((ROWS, D), f32),
            pltpu.VMEM((ROWS, D), bf16),
            pltpu.VMEM((ROWS, D), bf16),
            pltpu.VMEM((ROWS, D), f32),
            pltpu.VMEM((ROWS, D), f32),
            pltpu.VMEM((ROWS, D), f32),
            pltpu.VMEM((ROWS, D), f32),
            pltpu.VMEM((ROWS, D), bf16),
            pltpu.VMEM((ROWS, D), bf16),
            pltpu.VMEM((3, ROWS, D), bf16),
            pltpu.VMEM((WINDOWS, GROUPS, PAD, WIDE), f32),
            pltpu.SemaphoreType.DMA,
            pltpu.SemaphoreType.DMA,
        ],
        name="layer",
    )(slots, out_slots, images, cotangent, perm, small, bias, mask, *pieces)


VIEW = PIECE * D * 3 // 128


def shard_kinds(device):
    third = 3 * device + jnp.arange(3, dtype=jnp.int32)
    is_up = (third >= PROJ_END) & (third < UP_END)
    return jnp.where(third < QKV_END, 0, jnp.where(is_up, 2, 1)).astype(jnp.int32)


def piece_rows(kind, part):
    per_row = D // 128
    if kind == 0:
        return [(slice(0, PIECE), per_row * part, 3 * per_row)]
    if kind == 1:
        return [(slice(0, PIECE), per_row * PIECE * part, per_row)]
    return [
        (slice(j * UP_ROWS, (j + 1) * UP_ROWS), per_row * (PIECE * part + j), per_row * (FF // D))
        for j in range(FF // D)
    ]


def pack_kernel(kinds, shard, out):
    for part in range(3):
        for kind in range(3):

            @pl.when(kinds[part] == kind)
            def _(part=part, kind=kind):
                for rows, start, stride in piece_rows(kind, part):
                    size = rows.stop - rows.start
                    for lane in range(D // 128):
                        lanes = slice(lane * 128, (lane + 1) * 128)
                        value = shard[pl.ds(start + lane, size, stride=stride), :].astype(bf16)
                        out[part, rows, lanes] = value


def pack_shard(shard, kinds):
    vmem = pl.BlockSpec(memory_space=pltpu.VMEM)
    return pl.pallas_call(
        pack_kernel,
        in_specs=[pl.BlockSpec(memory_space=pltpu.SMEM), vmem],
        out_specs=vmem,
        out_shape=jax.ShapeDtypeStruct((3, PIECE, D), bf16),
        name="pack",
    )(kinds, shard.reshape(VIEW, 128))


def adam_step(weights, first_moment, second_moment, gradient, rate, decay):
    new_first = beta_one * first_moment + (1.0 - beta_one) * gradient
    new_second = beta_two * second_moment + (1.0 - beta_two) * gradient * gradient
    first_hat = new_first / (1.0 - beta_one**STEP)
    second_hat = new_second / (1.0 - beta_two**STEP)
    update = first_hat / (jnp.sqrt(second_hat) + adam_eps) + decay * weights
    return (weights - rate * update, new_first, new_second)


def adam_kernel(grad_scale):
    def body(kinds, *refs):
        mine, theirs, weights, first, second = refs[:5]
        grad, new_weights, new_first, new_second = refs[5:9]
        for part in range(3):
            for kind in range(3):

                @pl.when(kinds[part] == kind)
                def _(part=part, kind=kind):
                    for rows, start, stride in piece_rows(kind, part):
                        size = rows.stop - rows.start
                        for lane in range(D // 128):
                            lanes = slice(lane * 128, (lane + 1) * 128)
                            total = mine[part, rows, lanes].astype(f32) + theirs[
                                part, rows, lanes
                            ].astype(f32)
                            grad[pl.ds(start + lane, size, stride=stride), :] = total * grad_scale

        def step(number, carry):
            at = pl.ds(pl.multiple_of(number * 64, 64), 64)
            new_weights[at, :], new_first[at, :], new_second[at, :] = adam_step(
                weights[at, :], first[at, :], second[at, :], grad[at, :], rate_matrix, decay_rate
            )
            return carry

        lax.fori_loop(0, VIEW // 64, step, 0)

    return body


def adam_shard(kinds, parts, weights, first, second, grad_scale):
    vmem = pl.BlockSpec(memory_space=pltpu.VMEM)
    size = weights.shape[0]
    views = [
        pltpu.with_memory_space_constraint(array.reshape(VIEW, 128), pltpu.VMEM)
        for array in (weights, first, second)
    ]
    results = pl.pallas_call(
        adam_kernel(grad_scale),
        in_specs=[pl.BlockSpec(memory_space=pltpu.SMEM)] + [vmem] * 5,
        out_specs=[vmem] * 4,
        out_shape=[jax.ShapeDtypeStruct((VIEW, 128), f32)] * 4,
        name="adam",
    )(kinds, *parts, *views)
    return [result.reshape(size) for result in results]


def to_pieces(flat):
    q_end, p_end, u_end = QKV_END * PIECE * D, PROJ_END * PIECE * D, UP_END * PIECE * D
    qkv = flat[:q_end].reshape(-1, PIECE, 3, D).transpose(0, 2, 1, 3).reshape(-1, PIECE, D)
    proj = flat[q_end:p_end].reshape(-1, PIECE, D)
    up = flat[p_end:u_end].reshape(-1, UP_ROWS, FF // D, D).transpose(0, 2, 1, 3)
    down = flat[u_end:].reshape(-1, PIECE, D)
    return jnp.concatenate([qkv, proj, up.reshape(-1, PIECE, D), down])


def from_pieces(pieces):
    qkv = pieces[:QKV_END].reshape(-1, 3, PIECE, D).transpose(0, 2, 1, 3)
    up = pieces[PROJ_END:UP_END].reshape(-1, FF // D, UP_ROWS, D).transpose(0, 2, 1, 3)
    return jnp.concatenate(
        [
            qkv.reshape(-1),
            pieces[QKV_END:PROJ_END].reshape(-1),
            up.reshape(-1),
            pieces[UP_END:].reshape(-1),
        ]
    )


def offset_grid():
    spots = np.arange(PAD)
    rows_at = spots // WIN
    cols_at = spots % WIN
    grid = (rows_at[None, :] - rows_at[:, None] + WIN - 1) * (2 * WIN - 1) + (
        cols_at[None, :] - cols_at[:, None] + WIN - 1
    )
    real = (spots[:, None] < PLACES) & (spots[None, :] < PLACES)
    return np.where(real, grid, -1)


AXES = ("rep", "grp")


def on_device(
    images, cotangent, region_ids, rel_index, matrices, matrix_m, matrix_v, small, small_m, small_v
):
    devices = lax.axis_size("rep") * lax.axis_size("grp")
    me = lax.axis_index(AXES)
    bits = [1 << number for number in range(devices.bit_length() - 1)]
    exact = devices == sum(bits) + 1 and matrices.shape[0] == 3 * PIECE * D

    def swap(value, bit):
        return lax.ppermute(value, AXES, [(i, i ^ bit) for i in range(devices)])

    labels = jnp.arange(REL, dtype=jnp.int32)
    grid = jnp.asarray(offset_grid(), jnp.int32)

    def split(values):
        high = lax.reduce_precision(values, 8, 7)
        middle = lax.reduce_precision(values - high, 8, 7)
        low = values - high - middle
        return [part.astype(bf16) for part in (high, middle, low)]

    def tables(rel_index):
        select_offset = (grid[None] == labels[:, None, None]).astype(f32)
        select_row = (rel_index[:, None] == labels[None, :]).astype(f32)
        return select_offset, select_row

    def prepare(small, region_ids, rel_index):
        small_rows = small[: SMALL_ROWS * D].reshape(SMALL_ROWS, D)
        rel_table = small[SMALL_ROWS * D :].reshape(REL, HEADS)
        select_offset, select_row = tables(rel_index)
        table_rows = jnp.dot(select_row, rel_table, precision=highest)
        table_parts = jnp.concatenate(split(table_rows), axis=1)
        bias = jnp.einsum(
            "okq,oh->khq", select_offset.astype(bf16), table_parts, preferred_element_type=f32
        )
        bias = bias.reshape(PAD, 3, HEADS, PAD).sum(axis=1)
        blocks = SIDE // WIN
        regions = region_ids.reshape(blocks, WIN, blocks, WIN).transpose(0, 2, 1, 3)
        regions = regions.reshape(WINDOWS, PLACES)
        padded = ((0, 0), (0, PAD - PLACES))
        keys = jnp.pad(regions, padded, constant_values=-1)[:, :, None]
        queries = jnp.tile(jnp.pad(regions, padded, constant_values=-2), (1, GROUP))[:, None, :]
        mask = (keys == queries).astype(jnp.int32)
        return small_rows, bias.reshape(PAD, HEADS * PAD), mask

    if exact:
        core, inner, top = bits[0], bits[1:-1], bits[-1]
        orders = [inner[color:] + inner[:color] for color in range(3)]
        kinds = shard_kinds(me)
        packed = pack_shard(matrices, kinds)
        received = swap(packed, top)
        masks = [[0]] * 3 + [[top]] * 3
        for color in range(3):
            for step in range(1, len(inner)):
                for at in (color, 3 + color):
                    bit = orders[color][-step]
                    masks[at] = masks[at] + [mask ^ bit for mask in masks[at]]

        def slot_table(entries):
            table = jnp.asarray(entries, jnp.int32)
            return 3 * (me ^ table[:, 0]) + table[:, 1]

        out_entries = []
        for color in range(3):
            order = orders[color] + [top]
            half = [0]
            for bit in reversed(order[1:]):
                half = half + [mask ^ bit for mask in half]
            for extra in (order[0] ^ core, core, order[0], 0):
                out_entries += [(mask ^ extra, color) for mask in half]
        piece_entries = []
        for tree in range(2):
            for color in range(3):
                last = orders[color][0]
                for extra in (0, last, core, last ^ core):
                    piece_entries += [(mask ^ extra, color) for mask in masks[3 * tree + color]]
        operands = prepare(small, region_ids, rel_index)
        operands = (*operands, slot_table(piece_entries), slot_table(out_entries))
        received, operands = lax.optimization_barrier((received, operands))
        buffers = [tree[color : color + 1] for tree in (packed, received) for color in range(3)]
        for step, tree in ((1, 0), (1, 1), (2, 0), (2, 1)):
            for color in range(3):
                at = 3 * tree + color
                bit = orders[color][-step]
                own = buffers[at]
                other = swap(own, bit)
                buffers[at] = jnp.concatenate([own, other])

        pieces = []
        for tree in range(2):
            for color in range(3):
                buffer = buffers[3 * tree + color]
                far = swap(buffer, orders[color][0])
                pieces += [buffer, far, swap(buffer, core), swap(far, core)]
        outs = [devices // 4] * 12
    else:
        gathered = lax.all_gather(matrices.astype(bf16), AXES, axis=0, tiled=True)
        pieces = [to_pieces(gathered)]
        slots = jnp.arange(BLOCKS, dtype=jnp.int32)
        operands = (*prepare(small, region_ids, rel_index), slots, slots)
        outs = [BLOCKS]

    output, input_grad, sums, rel_sum, *grads = run_layer(
        images, cotangent, *operands, pieces, outs
    )

    tokens_all = images.shape[0] * devices * SIDE * SIDE
    grad_scale = 1.0 / math.sqrt(tokens_all)

    def small_sums(sums, rel_sum, rel_index):
        select_offset, select_row = tables(rel_index)
        rel_parts = jnp.concatenate(split(rel_sum.reshape(PAD, HEADS, PAD)), axis=1)
        rel_grad = jnp.einsum(
            "okq,khq->oh", select_offset.astype(bf16), rel_parts, preferred_element_type=f32
        )
        rel_grad = rel_grad.reshape(REL, 3, HEADS).sum(axis=1)
        table_grad = jnp.dot(select_row.T, rel_grad, precision=highest)
        return jnp.concatenate([sums.reshape(-1), table_grad.reshape(-1)]) * grad_scale

    if exact:

        def add(a, b):
            return (a.astype(f32) + b.astype(f32)).astype(bf16)

        from_far = [swap(grads[4 * color], core) for color in range(3)]
        from_near = [swap(grads[4 * color + 1], core) for color in range(3)]
        far = [add(grads[4 * color + 2], from_far[color]) for color in range(3)]
        small_grad = small_sums(sums, rel_sum, rel_index)
        near = [add(grads[4 * color + 3], from_near[color]) for color in range(3)]
        for stage in range(3):
            for color in range(3):
                received = swap(far[color], orders[color][stage])
                size = received.shape[0] // 2
                far[color] = add(near[color][size:], received[size:])
                near[color] = add(near[color][:size], received[:size])
        parts = [jnp.concatenate(near), swap(jnp.concatenate(far), top)]
        for bit in bits:
            small_grad = small_grad + swap(small_grad, bit)
        parts = [pltpu.with_memory_space_constraint(piece, pltpu.VMEM) for piece in parts]
        owned_grad, new_matrices, new_matrix_m, new_matrix_v = adam_shard(
            kinds, parts, matrices, matrix_m, matrix_v, grad_scale
        )
    else:
        flat_grad = from_pieces(grads[0].astype(f32)) * grad_scale
        owned_grad = lax.psum_scatter(flat_grad, AXES, scatter_dimension=0, tiled=True)
        new_matrices, new_matrix_m, new_matrix_v = adam_step(
            matrices, matrix_m, matrix_v, owned_grad, rate_matrix, decay_rate
        )
        small_grad = lax.psum(small_sums(sums, rel_sum, rel_index), AXES)
    new_small, new_small_m, new_small_v = adam_step(
        small, small_m, small_v, small_grad, rate_small, 0.0
    )
    return (
        output,
        input_grad,
        owned_grad,
        small_grad,
        new_matrices,
        new_matrix_m,
        new_matrix_v,
        new_small,
        new_small_m,
        new_small_v,
    )


def solution(mesh):
    tokens = P(AXES, None, None, None)
    shard = P(AXES)
    whole = P()

    return jax.shard_map(
        on_device,
        mesh=mesh,
        in_specs=(tokens, tokens, whole, whole, shard, shard, shard, whole, whole, whole),
        out_specs=(tokens, tokens, shard, whole, shard, shard, shard, whole, whole, whole),
        check_vma=False,
    )
```
